1024 devices in a mesh: pipe: 8 (over y_lo, core), ctx: 16 (over z, y_hi), tp: 8 (over x).
Axes of the slice: x: 8, y: 8 (y_hi: 2, y_lo: 4; y = y_hi * 4 + y_lo), z: 8, core: 2. Of those that a mesh axis runs over, the one named last changes fastest.
Arguments:
- queries: bfloat16 [8, 2048, 4096], P('pipe', 'ctx', 'tp'), may hold values from -15 to 15
- keys: bfloat16 [8, 2048, 1024], P('pipe', 'ctx', 'tp'), may hold values from -5 to 5
- values: bfloat16 [8, 2048, 1024], P('pipe', 'ctx', 'tp'), may hold values from -5 to 5
- span_ids: int32 [8, 32], P('pipe', 'ctx'), may hold values from 0 to 31, each once within a row
- cotangent: bfloat16 [8, 2048, 4096], P('pipe', 'ctx'), may hold values from -6 to 6
Outputs:
- attention: bfloat16 [8, 2048, 4096], P('pipe', 'ctx', 'tp')
- grad_out: bfloat16 [8, 4096, 4096], P('pipe', 'ctx', 'tp')
The draws below stay inside these ranges and needn't reach their ends.
Inputs may be any that keep to these rules, and one draw needn't show every extreme that they name: `span_ids`: each row is a permutation of 0 to 31.
All inputs are finite; a program needn't handle non-finite values.
Results may differ from the reference program's by a relative error of at most 0.015.
Values may be sent and summed in bfloat16 or wider, within the bound.
A program may use at most 32 MiB of HBM per device.

```python
import math
import jax
import jax.numpy as jnp
from jax import lax

HQ = 32
HK = 8
HD = 128
DW = 4096
TOK_DEV = 128
SPAN = 64
SPANS = 32
SEQ = 2048
N_PIPE = 8
N_CTX = 16


def drawn_pair(key):
    query_shape = (N_PIPE, SEQ, HQ * HD)
    key_shape = (N_PIPE, SEQ, HK * HD)
    query_draw = jnp.clip(jax.random.normal(jax.random.fold_in(key, 11), query_shape, jnp.float32), -4.0, 4.0)
    key_draw = jnp.clip(jax.random.normal(jax.random.fold_in(key, 12), key_shape, jnp.float32), -3.0, 3.0)
    return (query_draw, key_draw)


def draw_queries(key, part):
    return drawn_pair(key)[0].astype(jnp.bfloat16)


def draw_keys(key, part):
    return drawn_pair(key)[1].astype(jnp.bfloat16)


def with_spikes(drawn, own_key, source, target, parts, factor):
    def block_of(axis_at):
        return (jnp.arange(drawn.shape[axis_at]) // (drawn.shape[axis_at] // parts)).reshape((-1,) + (1,) * (drawn.ndim - 1 - axis_at))

    one_side = jax.random.permutation(own_key, parts)[block_of(target)]
    far = (block_of(target) + parts // 2) % parts
    return jnp.where((block_of(source) == one_side) | (block_of(source) == far), factor * drawn, drawn)


def level_of(own_key, shape, cuts, smallest, top_value):
    gain, own = 1.0, jax.random.fold_in(own_key, 6)
    for dim, shards_of in cuts:
        steps = jnp.exp(jax.random.uniform(jax.random.fold_in(own, dim), (shards_of,), jnp.float32, smallest / len(cuts), top_value / len(cuts)))
        gain = gain * jnp.repeat(steps, shape[dim] // shards_of).reshape([-1 if axis == dim else 1 for axis in range(len(shape))])
    return gain


def gaussian(own_key, shape, width, bound, cuts=(), kind=jnp.bfloat16):
    level = level_of(own_key, shape, cuts, -0.22, 0.18) if cuts else 1.0
    values = jax.random.normal(own_key, shape, jnp.float32) * width * level
    return jnp.minimum(jnp.maximum(values, -bound), bound).astype(kind)


def heavy_noise(stream_key, extent, deviation, bound, split, heavy, kind=jnp.bfloat16):
    entries = deviation * jax.random.normal(stream_key, extent, jnp.float32)
    if split:
        entries = entries * level_of(stream_key, extent, split, -0.22, 0.18)
    return jnp.clip(with_spikes(entries, jax.random.fold_in(stream_key, 3), *heavy), -bound, bound).astype(kind)


def setup_inputs(seed: int = 0) -> dict:
    key_list = jax.random.split(jax.random.key(seed), 6)
    return {
        "queries": draw_queries(jax.random.fold_in(key_list[5], 71), 0),
        "keys": draw_keys(jax.random.fold_in(key_list[5], 71), 0),
        "values": gaussian(key_list[2], (N_PIPE, SEQ, HK * HD), 1.0, 5.0, ((0, 8), (1, 16), (2, 8))),
        "span_ids": jax.vmap(lambda own: jax.random.permutation(own, SPANS))(jax.random.split(key_list[3], N_PIPE)).reshape((N_PIPE, SPANS)).astype(jnp.int32),
        "cotangent": heavy_noise(key_list[4], (N_PIPE, SEQ, DW), 1.0, 6.0, ((0, 8), (1, 16)), (1, 2, 16, 2.0)),
    }


def reference(queries, keys, values, span_ids, cotangent):
    rows = jnp.arange(SEQ, dtype=jnp.int32)
    group = HQ // HK
    scale = 1.0 / math.sqrt(HD)

    def one_batch(inputs):
        query_all, key_all, value_all, span_row, cot_all = inputs
        positions = span_row[rows // SPAN].astype(jnp.int32) * SPAN + rows % SPAN
        visible = positions[None, :] <= positions[:, None]
        query_heads = query_all.reshape(SEQ, HQ, HD).transpose(1, 0, 2)
        key_heads = key_all.reshape(SEQ, HK, HD).transpose(1, 0, 2)
        value_heads = value_all.reshape(SEQ, HK, HD).transpose(1, 0, 2)

        def one_head(head):
            query_one = query_heads[head]
            key_one = key_heads[head // group]
            value_one = value_heads[head // group]
            scores = jnp.dot(query_one, key_one.T, preferred_element_type=jnp.float32) * scale
            masked = jnp.where(visible, scores, -1e+30)
            top = lax.optimization_barrier(jnp.max(masked, axis=-1, keepdims=True))
            weights = jnp.where(visible, jnp.exp(scores - top), 0.0)
            total = lax.optimization_barrier(jnp.sum(weights, axis=-1))
            mixed = jnp.dot(weights.astype(jnp.bfloat16), value_one, preferred_element_type=jnp.float32)
            return mixed / total[:, None]
        outputs = lax.map(one_head, jnp.arange(HQ))
        attention = outputs.transpose(1, 0, 2).reshape(SEQ, HQ * HD).astype(jnp.bfloat16)
        blocks = attention.reshape(N_CTX, TOK_DEV, HQ * HD)
        cot_blocks = cot_all.reshape(N_CTX, TOK_DEV, DW)

        def add_block(summed, pair):
            att_block, cot_block = pair
            term = jnp.dot(cot_block.T, att_block, preferred_element_type=jnp.float32)
            term = lax.optimization_barrier(term.astype(jnp.bfloat16)).astype(jnp.float32)
            return (summed + term, None)
        summed = lax.scan(add_block, jnp.zeros((DW, HQ * HD), jnp.float32), (blocks, cot_blocks))[0]
        return (attention, summed)
    attention, summed = lax.map(one_batch, (queries, keys, values, span_ids, cotangent))
    grad_out = (summed + jnp.roll(summed, N_PIPE // 2, axis=0)).astype(jnp.bfloat16)
    return (attention, grad_out)
```

```python
import functools
import math

import jax
import jax.numpy as jnp
from jax import lax
from jax.experimental import pallas as pl
from jax.experimental.pallas import tpu as pltpu
from jax.sharding import PartitionSpec as P

HD = 128
PAD = 16
MESH = pl.DeviceIdType.MESH
BF = jnp.bfloat16
F32 = jnp.float32


class Ring:
    def __init__(self, n, long_right, ref_of, send, recv, right, left, first=None):
        self.n = n
        self.reach = n // 2 if long_right else (n - 1) // 2
        self.ref_of, self.send, self.recv = ref_of, send, recv
        self.right, self.left, self.first = right, left, first

    def copy(self, j):
        rightward = j <= self.reach
        source = j - 1 if rightward else (j + 1) % self.n
        src = self.ref_of(source, 0)
        if source == 0 and self.first is not None:
            src = self.first
        dst = self.ref_of(j, 1 if rightward else -1)
        return pltpu.make_async_remote_copy(
            src_ref=src,
            dst_ref=dst,
            send_sem=self.send(j),
            recv_sem=self.recv(j),
            device_id=self.right if rightward else self.left,
            device_id_type=MESH,
        )

    def landed(self, j):
        dst = self.ref_of(j, 0)
        rightward = j <= self.reach
        return pltpu.make_async_remote_copy(
            src_ref=dst,
            dst_ref=dst,
            send_sem=self.send(j),
            recv_sem=self.recv(j),
            device_id=self.right if rightward else self.left,
            device_id_type=MESH,
        )

    def begin(self):
        for j in sorted({1, self.n - 1}):
            self.copy(j).start()

    def step(self, s):
        slots = []
        if s <= self.reach:
            slots.append(s)
        if s <= self.n - 1 - self.reach:
            slots.append(self.n - s)
        for j in slots:
            self.landed(j).wait_recv()
            onward = j + 1 if j <= self.reach else j - 1
            if j <= self.reach and onward <= self.reach:
                self.copy(onward).start()
            elif j > self.reach and onward > self.reach:
                self.copy(onward).start()
        return slots

    def drain(self):
        for j in range(1, self.n):
            self.copy(j).wait_send()


def kernel(
    sizes, span, q, k, v, cot, att, grad,
    kbuf, vbuf, q4, scores, tops, probs, cbuf, cot_t, abuf, acc, out1, in1, out2, in2,
    kv_send, kv_recv, y_send, y_recv, a2a_send, a2a_recv, own_sem, x_send, x_recv, att_send, att_recv,
):
    n_pipe, nz, nx = sizes
    p, c, t = lax.axis_index("pipe"), lax.axis_index("ctx"), lax.axis_index("tp")
    side = lax.rem(c, 2)
    z = lax.div(c, 2)
    tokens = q.shape[0]
    heads = q.shape[1] // HD
    span_len = tokens // 2
    feats = cot.shape[1] // nz
    chunk = tokens // nx
    half = feats // 2

    def at_z(d):
        return {"ctx": lax.rem(z + d, nz) * 2 + side}

    def at_x(d):
        return {"tp": lax.rem(t + d, nx)}

    across = c + 1 - 2 * side
    mirror = lax.rem(p + n_pipe // 2, n_pipe)
    y_peer = {"ctx": across}
    fold_peer = {"pipe": mirror, "ctx": across}
    pair_peer = {"pipe": mirror}

    barrier = pltpu.get_barrier_semaphore()
    peers = [at_z(d) for d in range(1, nz)] + [y_peer, fold_peer, pair_peer, at_x(1), at_x(nx - 1)]
    for peer in peers:
        pl.semaphore_signal(barrier, inc=1, device_id=peer, device_id_type=MESH)

    lane = lax.broadcasted_iota(jnp.int32, (PAD, HD), 1)
    id0, id1 = span[0, 0].astype(F32), span[0, 1].astype(F32)
    kbuf[0, :tokens, :] = k[...]
    kbuf[0, tokens:, :] = jnp.where(lane < span_len, id0, id1).astype(BF)
    vbuf[0, :, :] = v[...]
    for h in range(heads):
        q4[h * tokens:(h + 1) * tokens, :] = q[:, h * HD:(h + 1) * HD]
    row = lax.broadcasted_iota(jnp.int32, (tokens, HD), 0)
    col = lax.broadcasted_iota(jnp.int32, (tokens, HD), 1)
    query_pos = jnp.where(row < span_len, id0, id1) * span_len + lax.rem(row, span_len).astype(F32)
    key_off = lax.rem(col, span_len).astype(F32)

    pl.semaphore_wait(barrier, len(peers))

    def z_ring(buf, base, g, long_right, first=None):
        return Ring(
            nz, long_right, lambda j, way: buf.at[base + j],
            lambda j: kv_send.at[g, j], lambda j: kv_recv.at[g, j], at_z(1), at_z(nz - 1), first,
        )

    k_own = z_ring(kbuf, 0, 0, True)
    v_own = z_ring(vbuf, 0, 1, False, v)
    k_far = z_ring(kbuf, nz, 2, False)
    v_far = z_ring(vbuf, nz, 3, True)
    k_over = pltpu.make_async_remote_copy(
        kbuf.at[0], kbuf.at[nz], y_send.at[0], y_recv.at[0], device_id=y_peer, device_id_type=MESH)
    v_over = pltpu.make_async_remote_copy(
        v, vbuf.at[nz], y_send.at[1], y_recv.at[1], device_id=y_peer, device_id_type=MESH)
    k_over.start()
    v_over.start()
    k_own.begin()
    v_own.begin()

    rows = pl.ds(pl.multiple_of(t * chunk, chunk), chunk)

    def to_z(d):
        columns = pl.ds(pl.multiple_of(lax.rem(z + d, nz) * feats, feats), feats)
        return cot.at[rows, columns]

    own_cot = pltpu.make_async_copy(to_z(0), cbuf.at[t, 0], own_sem)
    own_cot.start()
    a2a = {
        d: pltpu.make_async_remote_copy(
            to_z(d), cbuf.at[t, d], a2a_send.at[d], a2a_recv.at[d], device_id=at_z(d), device_id_type=MESH)
        for d in range(1, nz)
    }
    for d in sorted(a2a, key=lambda d: -min(d, nz - d)):
        a2a[d].start()

    factor = math.log2(math.e) / math.sqrt(HD)

    def score(slot):
        keys = kbuf[slot, :tokens, :]
        ids = kbuf[slot, tokens:, :].astype(F32)
        key_pos = jnp.broadcast_to(ids[0:1, :], (tokens, HD)) * span_len + key_off
        bias = jnp.where(key_pos <= query_pos, 0.0, -1e30)
        for h in range(heads):
            part = lax.dot_general(
                q4[h * tokens:(h + 1) * tokens, :], keys, (((1,), (1,)), ((), ())), preferred_element_type=F32)
            part = part * factor + bias
            scores[h, slot] = part
            tops[h] = part if slot == 0 else jnp.maximum(tops[h], part)

    score(0)
    steps = nz // 2
    x_steps = nx // 2
    for s in range(1, steps + 1):
        fresh = k_own.step(s)
        v_own.step(s)
        for slot in fresh:
            score(slot)
        if s == min(2, steps):
            k_over.wait_recv()
            k_far.begin()
            v_over.wait_recv()
            v_far.begin()
            score(nz)

    low, high = (0, nz // 2), (nz // 2, nz)

    def x_ring(g, part, long_right):
        def ref_of(j, way):
            place = lax.rem(t + way - j + 2 * nx, nx)
            return cbuf.at[place, part[0]:part[1]]

        return Ring(
            nx, long_right, ref_of, lambda j: x_send.at[g, j], lambda j: x_recv.at[g, j], at_x(1), at_x(nx - 1))

    x_low, x_high = x_ring(0, low, True), x_ring(1, high, False)
    own_cot.wait()
    for d in range(1, nz // 2):
        a2a[d].wait_recv()
    x_low.begin()
    for d in range(nz // 2, nz):
        a2a[d].wait_recv()
    x_high.begin()

    def x_step(s):
        if s <= x_steps:
            x_low.step(s)
            x_high.step(s)

    for s in range(1, steps + 1):
        fresh = k_far.step(s)
        v_far.step(s)
        for slot in fresh:
            score(nz + slot)
        if s == max(steps - 1, 1):
            x_step(1)

    a_rings = [
        Ring(
            nz, h % 2 == 0, functools.partial(lambda h, j, way: abuf.at[h, j], h),
            functools.partial(lambda h, j: att_send.at[h, j], h),
            functools.partial(lambda h, j: att_recv.at[h, j], h), at_z(1), at_z(nz - 1))
        for h in range(heads)
    ]

    def attend(h):
        top = jnp.broadcast_to(jnp.max(tops[h], axis=-1, keepdims=True), (tokens, HD))
        total = jnp.zeros((tokens, HD), F32)
        for slot in range(2 * nz):
            weights = jnp.exp2(scores[h, slot] - top)
            total = total + weights
            probs[:, slot * HD:(slot + 1) * HD] = weights.astype(BF)
        mixed = jnp.dot(probs[...], vbuf[...].reshape(2 * nz * tokens, HD), preferred_element_type=F32)
        out = (mixed / jnp.sum(total, axis=-1, keepdims=True)).astype(BF)
        abuf[h, 0] = out
        att[:, h * HD:(h + 1) * HD] = out

    for h in range(heads):
        attend(h)
        a_rings[h].begin()
        if h == 0:
            x_step(2)
        if h == heads - 1:
            x_step(3)

    def turn(j):
        block = cbuf[:, j].reshape(tokens, feats)
        cot_t[:, j * tokens:(j + 1) * tokens] = block.T

    for s in range(1, steps):
        for h in range(heads):
            a_rings[h].step(s)
        if s == 1:
            x_step(4)
        if s == min(2, steps - 1):
            for j in range(nz):
                turn(j)
    if steps == 1:
        x_step(4)
        for j in range(nz):
            turn(j)

    fold = [
        pltpu.make_async_remote_copy(
            out1.at[h, 1 - side], in1.at[h], y_send.at[2 + h], y_recv.at[2 + h],
            device_id=fold_peer, device_id_type=MESH)
        for h in range(heads)
    ]
    pair = [
        pltpu.make_async_remote_copy(
            out2.at[h], in2.at[h], y_send.at[2 + heads + h], y_recv.at[2 + heads + h],
            device_id=pair_peer, device_id_type=MESH)
        for h in range(heads)
    ]
    for h in range(heads):
        a_rings[h].step(steps)
        summed = jnp.dot(cot_t[...], abuf[h].reshape(nz * tokens, HD), preferred_element_type=F32)
        acc[h] = summed.reshape(2, half, HD)
        out1[h] = summed.astype(BF).reshape(2, half, HD)
        fold[h].start()
    for h in range(heads):
        fold[h].wait_recv()
        both = acc[h, side] + in1[h].astype(F32)
        acc[h, side] = both
        out2[h] = both.astype(BF)
        pair[h].start()
    for h in range(heads):
        pair[h].wait_recv()
        grad[:, h * HD:(h + 1) * HD] = (acc[h, side] + in2[h].astype(F32)).astype(BF)

    for ring in [k_own, v_own, k_far, v_far, x_low, x_high] + a_rings:
        ring.drain()
    for copy in [k_over, v_over] + list(a2a.values()) + fold + pair:
        copy.wait_send()


def solution(mesh):
    n_pipe, n_ctx, nx = mesh.shape["pipe"], mesh.shape["ctx"], mesh.shape["tp"]
    nz = n_ctx // 2

    def local(queries, keys, values, span_ids, cotangent):
        tokens, width = queries.shape[1:]
        heads = width // HD
        feats = cotangent.shape[2] // nz
        half = feats // 2
        dma = pltpu.SemaphoreType.DMA
        vmem = pl.BlockSpec(memory_space=pltpu.VMEM)
        attention, grad = pl.pallas_call(
            functools.partial(kernel, (n_pipe, nz, nx)),
            out_shape=(
                jax.ShapeDtypeStruct((tokens, width), BF),
                jax.ShapeDtypeStruct((half, width), BF),
            ),
            in_specs=[
                pl.BlockSpec(memory_space=pltpu.SMEM), vmem, vmem, vmem, pl.BlockSpec(memory_space=pl.ANY),
            ],
            out_specs=(vmem, vmem),
            scratch_shapes=[
                pltpu.VMEM((2 * nz, tokens + PAD, HD), BF),
                pltpu.VMEM((2 * nz, tokens, HD), BF),
                pltpu.VMEM((heads * tokens, HD), BF),
                pltpu.VMEM((heads, 2 * nz, tokens, HD), F32),
                pltpu.VMEM((heads, tokens, HD), F32),
                pltpu.VMEM((tokens, 2 * nz * HD), BF),
                pltpu.VMEM((nx, nz, tokens // nx, feats), BF),
                pltpu.VMEM((feats, nz * tokens), BF),
                pltpu.VMEM((heads, nz, tokens, HD), BF),
                pltpu.VMEM((heads, 2, half, HD), F32),
                pltpu.VMEM((heads, 2, half, HD), BF),
                pltpu.VMEM((heads, half, HD), BF),
                pltpu.VMEM((heads, half, HD), BF),
                pltpu.VMEM((heads, half, HD), BF),
                dma((4, nz)),
                dma((4, nz)),
                dma((2 + 2 * heads,)),
                dma((2 + 2 * heads,)),
                dma((nz,)),
                dma((nz,)),
                dma,
                dma((2, nx)),
                dma((2, nx)),
                dma((heads, nz)),
                dma((heads, nz)),
            ],
            compiler_params=pltpu.CompilerParams(
                collective_id=0, has_side_effects=True, vmem_limit_bytes=40 * 1024 * 1024
            ),
            name="fused",
        )(span_ids, queries[0], keys[0], values[0], cotangent[0])
        return attention[None], grad[None]

    return jax.shard_map(
        local,
        mesh=mesh,
        in_specs=(
            P("pipe", "ctx", "tp"),
            P("pipe", "ctx", "tp"),
            P("pipe", "ctx", "tp"),
            P("pipe", "ctx"),
            P("pipe", "ctx", None),
        ),
        out_specs=(P("pipe", "ctx", "tp"), P("pipe", "ctx", "tp")),
        check_vma=False,
    )
```

```python
import functools
import math

import jax
import jax.numpy as jnp
from jax import lax
from jax.experimental import pallas as pl
from jax.experimental.pallas import tpu as pltpu
from jax.sharding import PartitionSpec as P

HD = 128
PAD = 16
LAG = 1
MESH = pl.DeviceIdType.MESH
BF = jnp.bfloat16
F32 = jnp.float32


class Ring:
    def __init__(self, n, long_right, ref_of, blocks, send, recv, right, left):
        self.n = n
        self.reach = n // 2 if long_right else (n - 1) // 2
        self.ref_of, self.blocks, self.send, self.recv = ref_of, blocks, send, recv
        self.right, self.left = right, left

    def slots(self, s):
        return [s] * (s <= self.reach) + [self.n - s] * (s <= self.n - 1 - self.reach)

    def pass_to(self, j):
        rightward = j <= self.reach
        pltpu.make_async_remote_copy(
            src_ref=self.ref_of(j - 1 if rightward else (j + 1) % self.n, 0),
            dst_ref=self.ref_of(j, 1 if rightward else -1),
            send_sem=self.send,
            recv_sem=self.recv(j if rightward else self.n - j),
            device_id=self.right if rightward else self.left,
            device_id_type=MESH,
        ).start()

    def begin(self):
        for j in self.slots(1):
            self.pass_to(j)

    def forward(self, s):
        onward = self.slots(s + 1)
        for j in self.slots(s):
            if j <= self.reach and s + 1 in onward and s + 1 <= self.reach:
                self.pass_to(s + 1)
            elif j > self.reach and self.n - s - 1 in onward and self.n - s - 1 > self.reach:
                self.pass_to(self.n - s - 1)
        return self.slots(s)

    def step(self, s):
        settle(self.blocks(len(self.slots(s))), self.recv(s))
        return self.forward(s)


def settle(ref, sem):
    pltpu.make_async_copy(ref, ref, sem).wait()


def kernel(
    sizes, span_in, q, k, v, cot, att, grad,
    span, kbuf, vbuf, q4, scores, tops, probs, cbuf, cot_t, abuf, acc, out1, in1, out2, in2, last,
    sent, kv_recv, y_recv, a2a_recv, own_sem, x_recv, att_recv, in_sem, q_sem, att_sem, grad_sem,
):
    n_pipe, nz, nx = sizes
    p, c, t = lax.axis_index("pipe"), lax.axis_index("ctx"), lax.axis_index("tp")
    side = lax.rem(c, 2)
    z = lax.div(c, 2)
    tokens = q.shape[0]
    heads = q.shape[1] // HD
    span_len = tokens // 2
    feats = cot.shape[1] // nz
    chunk = tokens // nx
    half = feats // 2

    def at_z(d):
        return {"ctx": lax.rem(z + d, nz) * 2 + side}

    def at_x(d):
        return {"tp": lax.rem(t + d, nx)}

    across = c + 1 - 2 * side
    mirror = lax.rem(p + n_pipe // 2, n_pipe)
    y_peer = {"ctx": across}
    fold_peer = {"pipe": mirror, "ctx": across}
    pair_peer = {"pipe": mirror}

    barrier = pltpu.get_barrier_semaphore()
    peers = [at_z(d) for d in range(1, nz)] + [y_peer, fold_peer, pair_peer, at_x(1), at_x(nx - 1)]
    for peer in peers:
        pl.semaphore_signal(barrier, inc=1, device_id=peer, device_id_type=MESH)

    span_load = pltpu.make_async_copy(span_in, span, in_sem.at[0])
    k_load = pltpu.make_async_copy(k, kbuf.at[0, 0:tokens], in_sem.at[1])
    v_load = pltpu.make_async_copy(v, vbuf.at[0], in_sem.at[2])
    q_load = [
        pltpu.make_async_copy(
            q.at[:, h * HD:(h + 1) * HD], q4.at[h * tokens:(h + 1) * tokens, :], q_sem)
        for h in range(heads)
    ]
    for copy in [span_load, k_load, v_load] + q_load:
        copy.start()
    span_load.wait()
    lane = lax.broadcasted_iota(jnp.int32, (PAD, HD), 1)
    id0, id1 = span[0, 0].astype(F32), span[0, 1].astype(F32)
    kbuf[0, tokens:, :] = jnp.where(lane < span_len, id0, id1).astype(BF)
    k_load.wait()
    v_load.wait()
    pl.semaphore_wait(barrier, len(peers))

    def z_ring(buf, base, g, long_right):
        return Ring(
            nz, long_right, lambda j, way: buf.at[base + j], lambda count: buf.at[0:count],
            sent.at[g % 2], lambda s: kv_recv.at[g, s - 1], at_z(1), at_z(nz - 1),
        )

    k_own = z_ring(kbuf, 0, 0, True)
    v_own = z_ring(vbuf, 0, 1, False)
    k_far = z_ring(kbuf, nz, 2, False)
    v_far = z_ring(vbuf, nz, 3, True)
    k_over = pltpu.make_async_remote_copy(
        kbuf.at[0], kbuf.at[nz], sent.at[0], y_recv.at[0], device_id=y_peer, device_id_type=MESH)
    v_over = pltpu.make_async_remote_copy(
        vbuf.at[0], vbuf.at[nz], sent.at[1], y_recv.at[1], device_id=y_peer, device_id_type=MESH)
    k_own.begin()
    k_over.start()
    v_own.begin()
    v_over.start()

    rows = pl.ds(pl.multiple_of(t * chunk, chunk), chunk)

    def to_z(d):
        columns = pl.ds(pl.multiple_of(lax.rem(z + d, nz) * feats, feats), feats)
        return cot.at[rows, columns]

    own_cot = pltpu.make_async_copy(to_z(0), cbuf.at[t, 0], own_sem)
    own_cot.start()
    a2a = {
        d: pltpu.make_async_remote_copy(
            to_z(d), cbuf.at[t, d], sent.at[2], a2a_recv.at[d // (nz // 2)], device_id=at_z(d), device_id_type=MESH)
        for d in range(1, nz)
    }
    by_reach = {}
    for d in range(1, nz):
        by_reach.setdefault(min(d, nz - d), []).append(d)

    for reach in sorted(by_reach, reverse=True):
        for d in by_reach[reach]:
            a2a[d].start()

    row = lax.broadcasted_iota(jnp.int32, (tokens, HD), 0)
    col = lax.broadcasted_iota(jnp.int32, (tokens, HD), 1)
    query_pos = jnp.where(row < span_len, id0, id1) * span_len + lax.rem(row, span_len).astype(F32)
    key_off = lax.rem(col, span_len).astype(F32)

    settle(q4, q_sem)

    factor = math.log2(math.e) / math.sqrt(HD)

    def score(slot):
        keys = kbuf[slot, :tokens, :]
        ids = kbuf[slot, tokens:, :].astype(F32)
        key_pos = jnp.broadcast_to(ids[0:1, :], (tokens, HD)) * span_len + key_off
        bias = jnp.where(key_pos <= query_pos, 0.0, -1e30)
        for h in range(heads):
            part = lax.dot_general(
                q4[h * tokens:(h + 1) * tokens, :], keys, (((1,), (1,)), ((), ())), preferred_element_type=F32)
            part = part * factor + bias
            scores[h, slot] = part
            tops[h] = part if slot == 0 else jnp.maximum(tops[h], part)

    score(0)
    steps = nz // 2
    x_steps = nx // 2
    low, high = (0, nz // 2), (nz // 2, nz)

    def x_ring(part, long_right):
        def ref_of(j, way):
            place = lax.rem(t + way - j + 2 * nx, nx)
            return cbuf.at[place, part[0]:part[1]]

        return Ring(nx, long_right, ref_of, None, sent.at[3], lambda s: x_recv.at[s - 1], at_x(1), at_x(nx - 1))

    x_low, x_high = x_ring(low, True), x_ring(high, False)

    def x_step(s):
        if s <= x_steps:
            settle(cbuf.at[0:(len(x_low.slots(s)) + len(x_high.slots(s))) // 2], x_recv.at[s - 1])
            x_low.forward(s)
            x_high.forward(s)

    def own_step(s):
        fresh = k_own.step(s)
        v_own.step(s)
        return fresh

    def far_step(s):
        fresh = [nz + slot for slot in k_far.step(s)]
        v_far.step(s)
        return fresh

    def over():
        k_over.wait_recv()
        k_far.begin()
        v_over.wait_recv()
        v_far.begin()
        return [nz]

    def x_begin():
        own_cot.wait()
        settle(cbuf.at[t, 1:nz // 2], a2a_recv.at[0])
        x_low.begin()
        settle(cbuf.at[t, nz // 2:nz], a2a_recv.at[1])
        x_high.begin()

    lag = min(LAG, steps)
    for s in range(1, steps + lag + 1):
        fresh = []
        if s <= steps:
            fresh += own_step(s)
        if s == lag:
            fresh += over()
        if s > lag:
            fresh += far_step(s - lag)
        if s == 2:
            x_begin()
        if s == steps:
            x_step(1)
        for slot in fresh:
            score(slot)

    a_rings = [
        Ring(
            nz, h % 2 == 0, functools.partial(lambda h, j, way: abuf.at[h, j], h),
            functools.partial(lambda h, count: abuf.at[h, 0:count], h), sent.at[4],
            functools.partial(lambda h, s: att_recv.at[h, s - 1], h), at_z(1), at_z(nz - 1))
        for h in range(heads)
    ]

    def attend(h):
        top = jnp.broadcast_to(jnp.max(tops[h], axis=-1, keepdims=True), (tokens, HD))
        total = jnp.zeros((tokens, HD), F32)
        for slot in range(2 * nz):
            weights = jnp.exp2(scores[h, slot] - top)
            total = total + weights
            probs[:, slot * HD:(slot + 1) * HD] = weights.astype(BF)
        mixed = jnp.dot(probs[...], vbuf[...].reshape(2 * nz * tokens, HD), preferred_element_type=F32)
        out = (mixed / jnp.sum(total, axis=-1, keepdims=True)).astype(BF)
        abuf[h, 0] = out

    att_out = [
        pltpu.make_async_copy(abuf.at[h, 0], att.at[:, h * HD:(h + 1) * HD], att_sem) for h in range(heads)
    ]
    for h in range(heads):
        attend(h)
        a_rings[h].begin()
        if h == 1:
            x_step(2)
    for copy in att_out:
        copy.start()

    def turn(j):
        block = cbuf[:, j].reshape(tokens, feats)
        cot_t[:, j * tokens:(j + 1) * tokens] = block.T

    for s in range(1, steps):
        for h in range(heads):
            a_rings[h].step(s)
        if s == 1:
            x_step(3)
        if s == steps - 1:
            x_step(4)
    for j in range(nz):
        turn(j)

    fold = [
        pltpu.make_async_remote_copy(
            out1.at[h, 1 - side], in1.at[h], sent.at[5], y_recv.at[2 + h],
            device_id=fold_peer, device_id_type=MESH)
        for h in range(heads)
    ]
    pair = [
        pltpu.make_async_remote_copy(
            out2.at[h], in2.at[h], sent.at[6], y_recv.at[2 + heads + h],
            device_id=pair_peer, device_id_type=MESH)
        for h in range(heads)
    ]
    for h in range(heads):
        a_rings[h].step(steps)
        summed = jnp.dot(cot_t[...], abuf[h].reshape(nz * tokens, HD), preferred_element_type=F32)
        acc[h] = summed.reshape(2, half, HD)
        out1[h] = summed.astype(BF).reshape(2, half, HD)
        fold[h].start()
    for h in range(heads):
        fold[h].wait_recv()
        both = acc[h, side] + in1[h].astype(F32)
        acc[h, side] = both
        out2[h] = both.astype(BF)
        pair[h].start()
    grad_out = [
        pltpu.make_async_copy(last.at[h], grad.at[:, h * HD:(h + 1) * HD], grad_sem) for h in range(heads)
    ]
    for h in range(heads):
        pair[h].wait_recv()
        last[h] = (acc[h, side] + in2[h].astype(F32)).astype(BF)
        grad_out[h].start()

    for g, ref in enumerate(
        [kbuf.at[1:2 * nz], vbuf.at[1:2 * nz], cbuf.at[0, 1:nz], cbuf.at[0:nx - 1], abuf.at[:, 1:nz], in1, in2]
    ):
        settle(ref, sent.at[g])
    settle(att, att_sem)
    settle(grad, grad_sem)


def solution(mesh):
    n_pipe, n_ctx, nx = mesh.shape["pipe"], mesh.shape["ctx"], mesh.shape["tp"]
    nz = n_ctx // 2

    def local(queries, keys, values, span_ids, cotangent):
        tokens, width = queries.shape[1:]
        heads = width // HD
        feats = cotangent.shape[2] // nz
        half = feats // 2
        dma = pltpu.SemaphoreType.DMA
        hbm = pl.BlockSpec(memory_space=pltpu.HBM)
        attention, grad = pl.pallas_call(
            functools.partial(kernel, (n_pipe, nz, nx)),
            out_shape=(
                jax.ShapeDtypeStruct((tokens, width), BF),
                jax.ShapeDtypeStruct((half, width), BF),
            ),
            in_specs=[hbm] * 5,
            out_specs=(hbm, hbm),
            scratch_shapes=[
                pltpu.SMEM((1, 2), jnp.int32),
                pltpu.VMEM((2 * nz, tokens + PAD, HD), BF),
                pltpu.VMEM((2 * nz, tokens, HD), BF),
                pltpu.VMEM((heads * tokens, HD), BF),
                pltpu.VMEM((heads, 2 * nz, tokens, HD), F32),
                pltpu.VMEM((heads, tokens, HD), F32),
                pltpu.VMEM((tokens, 2 * nz * HD), BF),
                pltpu.VMEM((nx, nz, tokens // nx, feats), BF),
                pltpu.VMEM((feats, nz * tokens), BF),
                pltpu.VMEM((heads, nz, tokens, HD), BF),
                pltpu.VMEM((heads, 2, half, HD), F32),
                pltpu.VMEM((heads, 2, half, HD), BF),
                pltpu.VMEM((heads, half, HD), BF),
                pltpu.VMEM((heads, half, HD), BF),
                pltpu.VMEM((heads, half, HD), BF),
                pltpu.VMEM((heads, half, HD), BF),
                dma((7,)),
                dma((4, nz // 2)),
                dma((2 + 2 * heads,)),
                dma((2,)),
                dma,
                dma((nx // 2,)),
                dma((heads, nz // 2)),
                dma((3,)),
                dma,
                dma,
                dma,
            ],
            compiler_params=pltpu.CompilerParams(
                collective_id=0, has_side_effects=True, vmem_limit_bytes=41943040
            ),
            name="fused",
        )(*[pltpu.with_memory_space_constraint(a, pltpu.HBM) for a in (span_ids, queries[0], keys[0], values[0], cotangent[0])])
        return attention[None], grad[None]

    return jax.shard_map(
        local,
        mesh=mesh,
        in_specs=(
            P("pipe", "ctx", "tp"),
            P("pipe", "ctx", "tp"),
            P("pipe", "ctx", "tp"),
            P("pipe", "ctx"),
            P("pipe", "ctx", None),
        ),
        out_specs=(P("pipe", "ctx", "tp"), P("pipe", "ctx", "tp")),
        check_vma=False,
    )
```

```python
import functools
import math

import jax
import jax.numpy as jnp
from jax import lax
from jax.experimental import pallas as pl
from jax.experimental.pallas import tpu as pltpu
from jax.sharding import PartitionSpec as P

HD = 128
PAD = 16
MESH = pl.DeviceIdType.MESH
BF = jnp.bfloat16
F32 = jnp.float32


class Spread:
    def __init__(self, n, long_right, ref_of, blocks, send, recv, at):
        self.n = n
        self.reach = n // 2 if long_right else (n - 1) // 2
        self.ref_of, self.blocks, self.send, self.recv, self.at = ref_of, blocks, send, recv, at

    def slots(self, group):
        rightward = [j for j in range(1, self.reach + 1) if min(j, 3) == group]
        leftward = [self.n - d for d in range(1, self.n - self.reach) if min(d, 3) == group]
        return rightward + leftward

    def emit(self, group):
        for j in self.slots(group):
            rightward = j <= self.reach
            apart = j if rightward else self.n - j
            via = 2 if apart > 2 else 0
            hop = apart - via
            signed = hop if rightward else -hop
            source = via if rightward else (self.n - via) % self.n
            pltpu.make_async_remote_copy(
                src_ref=self.ref_of(source, 0),
                dst_ref=self.ref_of(j, signed),
                send_sem=self.send,
                recv_sem=self.recv(group),
                device_id=self.at(signed),
                device_id_type=MESH,
            ).start()

    def begin(self):
        self.emit(2)
        self.emit(1)

    def take(self, group):
        count = len(self.slots(group))
        if count:
            settle(self.blocks(count), self.recv(group))
        return self.slots(group)

    def relay(self):
        slots = self.take(2)
        self.emit(3)
        return slots


def settle(ref, sem):
    pltpu.make_async_copy(ref, ref, sem).wait()


def kernel(
    sizes, span_in, q, k, v, cot, att, grad,
    span, kbuf, vbuf, q4, scores, tops, probs, cbuf, cot_t, abuf, acc, out1, in1, out2, in2, last,
    sent, kv_recv, y_recv, a2a_recv, own_sem, x_recv, att_recv, in_sem, q_sem, att_sem, grad_sem,
):
    n_pipe, nz, nx = sizes
    p, c, t = lax.axis_index("pipe"), lax.axis_index("ctx"), lax.axis_index("tp")
    side = lax.rem(c, 2)
    z = lax.div(c, 2)
    tokens = q.shape[0]
    heads = q.shape[1] // HD
    span_len = tokens // 2
    feats = cot.shape[1] // nz
    chunk = tokens // nx
    half = feats // 2

    def at_z(d):
        return {"ctx": lax.rem(z + d + nz, nz) * 2 + side}

    def at_x(d):
        return {"tp": lax.rem(t + d + nx, nx)}

    across = c + 1 - 2 * side
    mirror = lax.rem(p + n_pipe // 2, n_pipe)
    y_peer = {"ctx": across}
    fold_peer = {"pipe": mirror, "ctx": across}
    pair_peer = {"pipe": mirror}

    barrier = pltpu.get_barrier_semaphore()
    peers = [at_z(d) for d in range(1, nz)] + [y_peer, fold_peer, pair_peer]
    peers += [at_x(d) for d in sorted({hop % nx for hop in (-2, -1, 1, 2)} - {0})]
    for peer in peers:
        pl.semaphore_signal(barrier, inc=1, device_id=peer, device_id_type=MESH)

    span_load = pltpu.make_async_copy(span_in, span, in_sem.at[0])
    k_load = pltpu.make_async_copy(k, kbuf.at[0, 0:tokens], in_sem.at[1])
    v_load = pltpu.make_async_copy(v, vbuf.at[0], in_sem.at[2])
    q_load = [
        pltpu.make_async_copy(
            q.at[:, h * HD:(h + 1) * HD], q4.at[h * tokens:(h + 1) * tokens, :], q_sem)
        for h in range(heads)
    ]
    for copy in [span_load, k_load, v_load] + q_load:
        copy.start()
    span_load.wait()
    lane = lax.broadcasted_iota(jnp.int32, (PAD, HD), 1)
    id0, id1 = span[0, 0].astype(F32), span[0, 1].astype(F32)
    kbuf[0, tokens:, :] = jnp.where(lane < span_len, id0, id1).astype(BF)
    k_load.wait()
    v_load.wait()
    pl.semaphore_wait(barrier, len(peers))

    def z_ring(buf, base, g, long_right):
        return Spread(
            nz, long_right, lambda j, way: buf.at[base + j], lambda count: buf.at[0:count],
            sent.at[g % 2], lambda group: kv_recv.at[g, group - 1], at_z,
        )

    k_own = z_ring(kbuf, 0, 0, True)
    v_own = z_ring(vbuf, 0, 1, False)
    k_far = z_ring(kbuf, nz, 2, False)
    v_far = z_ring(vbuf, nz, 3, True)
    k_over = pltpu.make_async_remote_copy(
        kbuf.at[0], kbuf.at[nz], sent.at[0], y_recv.at[0], device_id=y_peer, device_id_type=MESH)
    v_over = pltpu.make_async_remote_copy(
        vbuf.at[0], vbuf.at[nz], sent.at[1], y_recv.at[1], device_id=y_peer, device_id_type=MESH)
    k_own.begin()
    k_over.start()
    v_own.begin()
    v_over.start()

    rows = pl.ds(pl.multiple_of(t * chunk, chunk), chunk)

    def to_z(d):
        columns = pl.ds(pl.multiple_of(lax.rem(z + d, nz) * feats, feats), feats)
        return cot.at[rows, columns]

    own_cot = pltpu.make_async_copy(to_z(0), cbuf.at[t, 0], own_sem)
    own_cot.start()
    a2a = {
        d: pltpu.make_async_remote_copy(
            to_z(d), cbuf.at[t, d], sent.at[2], a2a_recv.at[d // (nz // 2)], device_id=at_z(d), device_id_type=MESH)
        for d in range(1, nz)
    }
    by_reach = {}
    for d in range(1, nz):
        by_reach.setdefault(min(d, nz - d), []).append(d)

    for reach in sorted(by_reach, reverse=True):
        for d in by_reach[reach]:
            a2a[d].start()

    row = lax.broadcasted_iota(jnp.int32, (tokens, HD), 0)
    col = lax.broadcasted_iota(jnp.int32, (tokens, HD), 1)
    query_pos = jnp.where(row < span_len, id0, id1) * span_len + lax.rem(row, span_len).astype(F32)
    key_off = lax.rem(col, span_len).astype(F32)

    settle(q4, q_sem)

    factor = math.log2(math.e) / math.sqrt(HD)

    def score(slot):
        keys = kbuf[slot, :tokens, :]
        ids = kbuf[slot, tokens:, :].astype(F32)
        key_pos = jnp.broadcast_to(ids[0:1, :], (tokens, HD)) * span_len + key_off
        bias = jnp.where(key_pos <= query_pos, 0.0, -1e30)
        for h in range(heads):
            part = lax.dot_general(
                q4[h * tokens:(h + 1) * tokens, :], keys, (((1,), (1,)), ((), ())), preferred_element_type=F32)
            part = part * factor + bias
            scores[h, slot] = part
            tops[h] = part if slot == 0 else jnp.maximum(tops[h], part)

    score(0)
    low, high = (0, nz // 2), (nz // 2, nz)

    def x_ring(part, long_right):
        def ref_of(j, way):
            place = lax.rem(t + way - j + 2 * nx, nx)
            return cbuf.at[place, part[0]:part[1]]

        return Spread(nx, long_right, ref_of, None, sent.at[3], lambda group: x_recv.at[group - 1], at_x)

    x_low, x_high = x_ring(low, True), x_ring(high, False)

    def x_take(group):
        count = len(x_low.slots(group)) + len(x_high.slots(group))
        if count:
            settle(cbuf.at[0:count // 2], x_recv.at[group - 1])

    fresh = k_own.relay()
    v_own.relay()
    k_over.wait_recv()
    k_far.begin()
    v_over.wait_recv()
    v_far.begin()
    for slot in fresh + k_own.take(1) + [nz]:
        score(slot)
    own_cot.wait()
    settle(cbuf.at[t, 1:nz // 2], a2a_recv.at[0])
    x_low.begin()
    settle(cbuf.at[t, nz // 2:nz], a2a_recv.at[1])
    x_high.begin()
    for slot in k_own.take(3):
        score(slot)
    fresh = k_far.relay()
    v_far.relay()
    for slot in fresh + k_far.take(1):
        score(nz + slot)
    x_take(2)
    x_low.emit(3)
    x_high.emit(3)
    for slot in k_far.take(3):
        score(nz + slot)
    v_own.take(1)
    v_own.take(3)
    v_far.take(1)
    v_far.take(3)

    a_rings = [
        Spread(
            nz, h % 2 == 0, functools.partial(lambda h, j, way: abuf.at[h, j], h),
            functools.partial(lambda h, count: abuf.at[h, 0:count], h), sent.at[4],
            functools.partial(lambda h, group: att_recv.at[h, group - 1], h), at_z)
        for h in range(heads)
    ]

    def attend(h):
        top = jnp.broadcast_to(jnp.max(tops[h], axis=-1, keepdims=True), (tokens, HD))
        total = jnp.zeros((tokens, HD), F32)
        for slot in range(2 * nz):
            weights = jnp.exp2(scores[h, slot] - top)
            total = total + weights
            probs[:, slot * HD:(slot + 1) * HD] = weights.astype(BF)
        mixed = jnp.dot(probs[...], vbuf[...].reshape(2 * nz * tokens, HD), preferred_element_type=F32)
        out = (mixed / jnp.sum(total, axis=-1, keepdims=True)).astype(BF)
        abuf[h, 0] = out

    att_out = [
        pltpu.make_async_copy(abuf.at[h, 0], att.at[:, h * HD:(h + 1) * HD], att_sem) for h in range(heads)
    ]
    for h in range(heads):
        attend(h)
        a_rings[h].begin()
    for copy in att_out:
        copy.start()

    def turn(j):
        block = cbuf[:, j].reshape(tokens, feats)
        cot_t[:, j * tokens:(j + 1) * tokens] = block.T

    x_take(1)
    x_take(3)
    for j in range(nz):
        turn(j)
    for h in range(heads):
        a_rings[h].relay()
    for h in range(heads):
        a_rings[h].take(1)

    fold = [
        pltpu.make_async_remote_copy(
            out1.at[h, 1 - side], in1.at[h], sent.at[5], y_recv.at[2 + h],
            device_id=fold_peer, device_id_type=MESH)
        for h in range(heads)
    ]
    pair = [
        pltpu.make_async_remote_copy(
            out2.at[h], in2.at[h], sent.at[6], y_recv.at[2 + heads + h],
            device_id=pair_peer, device_id_type=MESH)
        for h in range(heads)
    ]
    for h in range(heads):
        a_rings[h].take(3)
        summed = jnp.dot(cot_t[...], abuf[h].reshape(nz * tokens, HD), preferred_element_type=F32)
        acc[h] = summed.reshape(2, half, HD)
        out1[h] = summed.astype(BF).reshape(2, half, HD)
        fold[h].start()
    for h in range(heads):
        fold[h].wait_recv()
        both = acc[h, side] + in1[h].astype(F32)
        acc[h, side] = both
        out2[h] = both.astype(BF)
        pair[h].start()
    grad_out = [
        pltpu.make_async_copy(last.at[h], grad.at[:, h * HD:(h + 1) * HD], grad_sem) for h in range(heads)
    ]
    for h in range(heads):
        pair[h].wait_recv()
        last[h] = (acc[h, side] + in2[h].astype(F32)).astype(BF)
        grad_out[h].start()

    for g, ref in enumerate(
        [kbuf.at[1:2 * nz], vbuf.at[1:2 * nz], cbuf.at[0, 1:nz], cbuf.at[0:nx - 1], abuf.at[:, 1:nz], in1, in2]
    ):
        settle(ref, sent.at[g])
    settle(att, att_sem)
    settle(grad, grad_sem)


def solution(mesh):
    n_pipe, n_ctx, nx = mesh.shape["pipe"], mesh.shape["ctx"], mesh.shape["tp"]
    nz = n_ctx // 2

    def local(queries, keys, values, span_ids, cotangent):
        tokens, width = queries.shape[1:]
        heads = width // HD
        feats = cotangent.shape[2] // nz
        half = feats // 2
        dma = pltpu.SemaphoreType.DMA
        hbm = pl.BlockSpec(memory_space=pltpu.HBM)
        attention, grad = pl.pallas_call(
            functools.partial(kernel, (n_pipe, nz, nx)),
            out_shape=(
                jax.ShapeDtypeStruct((tokens, width), BF),
                jax.ShapeDtypeStruct((half, width), BF),
            ),
            in_specs=[hbm] * 5,
            out_specs=(hbm, hbm),
            scratch_shapes=[
                pltpu.SMEM((1, 2), jnp.int32),
                pltpu.VMEM((2 * nz, tokens + PAD, HD), BF),
                pltpu.VMEM((2 * nz, tokens, HD), BF),
                pltpu.VMEM((heads * tokens, HD), BF),
                pltpu.VMEM((heads, 2 * nz, tokens, HD), F32),
                pltpu.VMEM((heads, tokens, HD), F32),
                pltpu.VMEM((tokens, 2 * nz * HD), BF),
                pltpu.VMEM((nx, nz, tokens // nx, feats), BF),
                pltpu.VMEM((feats, nz * tokens), BF),
                pltpu.VMEM((heads, nz, tokens, HD), BF),
                pltpu.VMEM((heads, 2, half, HD), F32),
                pltpu.VMEM((heads, 2, half, HD), BF),
                pltpu.VMEM((heads, half, HD), BF),
                pltpu.VMEM((heads, half, HD), BF),
                pltpu.VMEM((heads, half, HD), BF),
                pltpu.VMEM((heads, half, HD), BF),
                dma((7,)),
                dma((4, 3)),
                dma((2 + 2 * heads,)),
                dma((2,)),
                dma,
                dma((3,)),
                dma((heads, 3)),
                dma((3,)),
                dma,
                dma,
                dma,
            ],
            compiler_params=pltpu.CompilerParams(
                collective_id=0, has_side_effects=True, vmem_limit_bytes=41943040
            ),
            name="fused",
        )(*[pltpu.with_memory_space_constraint(a, pltpu.HBM) for a in (span_ids, queries[0], keys[0], values[0], cotangent[0])])
        return attention[None], grad[None]

    return jax.shard_map(
        local,
        mesh=mesh,
        in_specs=(
            P("pipe", "ctx", "tp"),
            P("pipe", "ctx", "tp"),
            P("pipe", "ctx", "tp"),
            P("pipe", "ctx"),
            P("pipe", "ctx", None),
        ),
        out_specs=(P("pipe", "ctx", "tp"), P("pipe", "ctx", "tp")),
        check_vma=False,
    )
```

```python
import functools
import math

import jax
import jax.numpy as jnp
from jax import lax
from jax.experimental import pallas as pl
from jax.experimental.pallas import tpu as pltpu
from jax.sharding import PartitionSpec as P

HD = 128
PAD = 16
MESH = pl.DeviceIdType.MESH
BF = jnp.bfloat16
F32 = jnp.float32


class Spread:
    def __init__(self, n, long_right, ref_of, blocks, send, recv, at, straight=False):
        self.straight = straight
        self.n = n
        self.reach = n // 2 if long_right else (n - 1) // 2
        self.ref_of, self.blocks, self.send, self.recv, self.at = ref_of, blocks, send, recv, at

    def slots(self, group):
        rightward = [j for j in range(1, self.reach + 1) if min(j, 3) == group]
        leftward = [self.n - d for d in range(1, self.n - self.reach) if min(d, 3) == group]
        return rightward + leftward

    def emit(self, group):
        for j in self.slots(group):
            rightward = j <= self.reach
            apart = j if rightward else self.n - j
            via = 2 if apart > 2 else 0 if self.straight else apart - 1
            hop = apart - via
            signed = hop if rightward else -hop
            source = via if rightward else (self.n - via) % self.n
            pltpu.make_async_remote_copy(
                src_ref=self.ref_of(source, 0),
                dst_ref=self.ref_of(j, signed),
                send_sem=self.send,
                recv_sem=self.recv(group),
                device_id=self.at(signed),
                device_id_type=MESH,
            ).start()

    def begin(self):
        if self.straight:
            self.emit(2)
        self.emit(1)

    def take(self, group):
        count = len(self.slots(group))
        if count:
            settle(self.blocks(count), self.recv(group))
        return self.slots(group)

    def relay(self, group):
        slots = self.take(group)
        self.emit(group + 1)
        return slots


def settle(ref, sem):
    pltpu.make_async_copy(ref, ref, sem).wait()


def kernel(
    sizes, span_in, q, k, v, cot, att, grad,
    span, kbuf, vbuf, q4, scores, tops, probs, cbuf, cot_t, abuf, acc, out1, in1, out2, in2, last,
    sent, kv_recv, y_recv, a2a_recv, own_sem, x_recv, att_recv, in_sem, q_sem, att_sem, grad_sem,
):
    n_pipe, nz, nx = sizes
    p, c, t = lax.axis_index("pipe"), lax.axis_index("ctx"), lax.axis_index("tp")
    side = lax.rem(c, 2)
    z = lax.div(c, 2)
    tokens = q.shape[0]
    heads = q.shape[1] // HD
    span_len = tokens // 2
    feats = cot.shape[1] // nz
    chunk = tokens // nx
    half = feats // 2

    def at_z(d):
        return {"ctx": lax.rem(z + d + nz, nz) * 2 + side}

    def at_x(d):
        return {"tp": lax.rem(t + d + nx, nx)}

    across = c + 1 - 2 * side
    mirror = lax.rem(p + n_pipe // 2, n_pipe)
    y_peer = {"ctx": across}
    fold_peer = {"pipe": mirror, "ctx": across}
    pair_peer = {"pipe": mirror}

    barrier = pltpu.get_barrier_semaphore()
    peers = [at_z(d) for d in range(1, nz)] + [y_peer, fold_peer, pair_peer]
    peers += [at_x(d) for d in sorted({hop % nx for hop in (-2, -1, 1, 2)} - {0})]
    for peer in peers:
        pl.semaphore_signal(barrier, inc=1, device_id=peer, device_id_type=MESH)

    span_load = pltpu.make_async_copy(span_in, span, in_sem.at[0])
    k_load = pltpu.make_async_copy(k, kbuf.at[0, 0:tokens], in_sem.at[1])
    v_load = pltpu.make_async_copy(v, vbuf.at[0], in_sem.at[2])
    q_load = [
        pltpu.make_async_copy(
            q.at[:, h * HD:(h + 1) * HD], q4.at[h * tokens:(h + 1) * tokens, :], q_sem)
        for h in range(heads)
    ]
    for copy in [span_load, k_load, v_load] + q_load:
        copy.start()
    span_load.wait()
    lane = lax.broadcasted_iota(jnp.int32, (PAD, HD), 1)
    id0, id1 = span[0, 0].astype(F32), span[0, 1].astype(F32)
    kbuf[0, tokens:, :] = jnp.where(lane < span_len, id0, id1).astype(BF)
    k_load.wait()
    v_load.wait()
    pl.semaphore_wait(barrier, len(peers))

    def z_ring(buf, base, g, long_right):
        return Spread(
            nz, long_right, lambda j, way: buf.at[base + j], lambda count: buf.at[0:count],
            sent.at[g % 2], lambda group: kv_recv.at[g, group - 1], at_z,
        )

    k_own = z_ring(kbuf, 0, 0, True)
    v_own = z_ring(vbuf, 0, 1, False)
    k_far = z_ring(kbuf, nz, 2, False)
    v_far = z_ring(vbuf, nz, 3, True)
    k_over = pltpu.make_async_remote_copy(
        kbuf.at[0], kbuf.at[nz], sent.at[0], y_recv.at[0], device_id=y_peer, device_id_type=MESH)
    v_over = pltpu.make_async_remote_copy(
        vbuf.at[0], vbuf.at[nz], sent.at[1], y_recv.at[1], device_id=y_peer, device_id_type=MESH)
    k_own.begin()
    k_over.start()
    v_own.begin()
    v_over.start()

    rows = pl.ds(pl.multiple_of(t * chunk, chunk), chunk)

    def to_z(d):
        columns = pl.ds(pl.multiple_of(lax.rem(z + d, nz) * feats, feats), feats)
        return cot.at[rows, columns]

    own_cot = pltpu.make_async_copy(to_z(0), cbuf.at[t, 0], own_sem)
    own_cot.start()
    a2a = {
        d: pltpu.make_async_remote_copy(
            to_z(d), cbuf.at[t, d], sent.at[2], a2a_recv.at[d // (nz // 2)], device_id=at_z(d), device_id_type=MESH)
        for d in range(1, nz)
    }
    by_reach = {}
    for d in range(1, nz):
        by_reach.setdefault(min(d, nz - d), []).append(d)

    for reach in sorted(by_reach, reverse=True):
        for d in by_reach[reach]:
            a2a[d].start()
    row = lax.broadcasted_iota(jnp.int32, (tokens, HD), 0)
    col = lax.broadcasted_iota(jnp.int32, (tokens, HD), 1)
    query_pos = jnp.where(row < span_len, id0, id1) * span_len + lax.rem(row, span_len).astype(F32)
    key_off = lax.rem(col, span_len).astype(F32)

    settle(q4, q_sem)

    factor = math.log2(math.e) / math.sqrt(HD)

    def score(slot):
        keys = kbuf[slot, :tokens, :]
        ids = kbuf[slot, tokens:, :].astype(F32)
        key_pos = jnp.broadcast_to(ids[0:1, :], (tokens, HD)) * span_len + key_off
        bias = jnp.where(key_pos <= query_pos, 0.0, -1e30)
        for h in range(heads):
            part = lax.dot_general(
                q4[h * tokens:(h + 1) * tokens, :], keys, (((1,), (1,)), ((), ())), preferred_element_type=F32)
            part = part * factor + bias
            scores[h, slot] = part
            tops[h] = part if slot == 0 else jnp.maximum(tops[h], part)

    score(0)
    low, high = (0, nz // 2), (nz // 2, nz)

    def x_ring(part, long_right):
        def ref_of(j, way):
            place = lax.rem(t + way - j + 2 * nx, nx)
            return cbuf.at[place, part[0]:part[1]]

        return Spread(nx, long_right, ref_of, None, sent.at[3], lambda group: x_recv.at[group - 1], at_x, True)

    x_low, x_high = x_ring(low, True), x_ring(high, False)

    def x_take(group):
        count = len(x_low.slots(group)) + len(x_high.slots(group))
        if count:
            settle(cbuf.at[0:count // 2], x_recv.at[group - 1])

    fresh = k_own.relay(1)
    v_own.relay(1)
    k_over.wait_recv()
    k_far.begin()
    v_over.wait_recv()
    v_far.begin()
    for slot in fresh + [nz]:
        score(slot)
    fresh = k_own.relay(2)
    v_own.relay(2)
    for slot in fresh:
        score(slot)
    fresh = k_far.relay(1)
    v_far.relay(1)
    for slot in fresh:
        score(nz + slot)
    own_cot.wait()
    settle(cbuf.at[t, 1:nz // 2], a2a_recv.at[0])
    x_low.begin()
    settle(cbuf.at[t, nz // 2:nz], a2a_recv.at[1])
    x_high.begin()
    fresh = k_far.relay(2)
    v_far.relay(2)
    for slot in fresh:
        score(nz + slot)
    for slot in k_own.take(3):
        score(slot)
    for slot in k_far.take(3):
        score(nz + slot)
    v_own.take(3)
    v_far.take(3)

    a_rings = [
        Spread(
            nz, h % 2 == 0, functools.partial(lambda h, j, way: abuf.at[h, j], h),
            functools.partial(lambda h, count: abuf.at[h, 0:count], h), sent.at[4],
            functools.partial(lambda h, group: att_recv.at[h, group - 1], h), at_z)
        for h in range(heads)
    ]

    def attend(h):
        top = jnp.broadcast_to(jnp.max(tops[h], axis=-1, keepdims=True), (tokens, HD))
        total = jnp.zeros((tokens, HD), F32)
        for slot in range(2 * nz):
            weights = jnp.exp2(scores[h, slot] - top)
            total = total + weights
            probs[:, slot * HD:(slot + 1) * HD] = weights.astype(BF)
        mixed = jnp.dot(probs[...], vbuf[...].reshape(2 * nz * tokens, HD), preferred_element_type=F32)
        out = (mixed / jnp.sum(total, axis=-1, keepdims=True)).astype(BF)
        abuf[h, 0] = out

    att_out = [
        pltpu.make_async_copy(abuf.at[h, 0], att.at[:, h * HD:(h + 1) * HD], att_sem) for h in range(heads)
    ]
    for h in range(heads):
        attend(h)
        a_rings[h].begin()
    x_take(2)
    x_low.emit(3)
    x_high.emit(3)
    for copy in att_out:
        copy.start()

    def turn(j):
        block = cbuf[:, j].reshape(tokens, feats)
        cot_t[:, j * tokens:(j + 1) * tokens] = block.T

    for h in range(heads):
        a_rings[h].relay(1)
    for h in range(heads):
        a_rings[h].relay(2)
    x_take(1)
    x_take(3)
    for j in range(nz):
        turn(j)

    fold = [
        pltpu.make_async_remote_copy(
            out1.at[h, 1 - side], in1.at[h], sent.at[5], y_recv.at[2 + h],
            device_id=fold_peer, device_id_type=MESH)
        for h in range(heads)
    ]
    pair = [
        pltpu.make_async_remote_copy(
            out2.at[h], in2.at[h], sent.at[6], y_recv.at[2 + heads + h],
            device_id=pair_peer, device_id_type=MESH)
        for h in range(heads)
    ]
    for h in range(heads):
        a_rings[h].take(3)
        summed = jnp.dot(cot_t[...], abuf[h].reshape(nz * tokens, HD), preferred_element_type=F32)
        acc[h] = summed.reshape(2, half, HD)
        out1[h] = summed.astype(BF).reshape(2, half, HD)
        fold[h].start()
    for h in range(heads):
        fold[h].wait_recv()
        both = acc[h, side] + in1[h].astype(F32)
        acc[h, side] = both
        out2[h] = both.astype(BF)
        pair[h].start()
    grad_out = [
        pltpu.make_async_copy(last.at[h], grad.at[:, h * HD:(h + 1) * HD], grad_sem) for h in range(heads)
    ]
    for h in range(heads):
        pair[h].wait_recv()
        last[h] = (acc[h, side] + in2[h].astype(F32)).astype(BF)
        grad_out[h].start()

    for g, ref in enumerate(
        [kbuf.at[1:2 * nz], vbuf.at[1:2 * nz], cbuf.at[0, 1:nz], cbuf.at[0:nx - 1], abuf.at[:, 1:nz], in1, in2]
    ):
        settle(ref, sent.at[g])
    settle(att, att_sem)
    settle(grad, grad_sem)


def solution(mesh):
    n_pipe, n_ctx, nx = mesh.shape["pipe"], mesh.shape["ctx"], mesh.shape["tp"]
    nz = n_ctx // 2

    def local(queries, keys, values, span_ids, cotangent):
        tokens, width = queries.shape[1:]
        heads = width // HD
        feats = cotangent.shape[2] // nz
        half = feats // 2
        dma = pltpu.SemaphoreType.DMA
        hbm = pl.BlockSpec(memory_space=pltpu.HBM)
        attention, grad = pl.pallas_call(
            functools.partial(kernel, (n_pipe, nz, nx)),
            out_shape=(
                jax.ShapeDtypeStruct((tokens, width), BF),
                jax.ShapeDtypeStruct((half, width), BF),
            ),
            in_specs=[hbm] * 5,
            out_specs=(hbm, hbm),
            scratch_shapes=[
                pltpu.SMEM((1, 2), jnp.int32),
                pltpu.VMEM((2 * nz, tokens + PAD, HD), BF),
                pltpu.VMEM((2 * nz, tokens, HD), BF),
                pltpu.VMEM((heads * tokens, HD), BF),
                pltpu.VMEM((heads, 2 * nz, tokens, HD), F32),
                pltpu.VMEM((heads, tokens, HD), F32),
                pltpu.VMEM((tokens, 2 * nz * HD), BF),
                pltpu.VMEM((nx, nz, tokens // nx, feats), BF),
                pltpu.VMEM((feats, nz * tokens), BF),
                pltpu.VMEM((heads, nz, tokens, HD), BF),
                pltpu.VMEM((heads, 2, half, HD), F32),
                pltpu.VMEM((heads, 2, half, HD), BF),
                pltpu.VMEM((heads, half, HD), BF),
                pltpu.VMEM((heads, half, HD), BF),
                pltpu.VMEM((heads, half, HD), BF),
                pltpu.VMEM((heads, half, HD), BF),
                dma((7,)),
                dma((4, 3)),
                dma((2 + 2 * heads,)),
                dma((2,)),
                dma,
                dma((3,)),
                dma((heads, 3)),
                dma((3,)),
                dma,
                dma,
                dma,
            ],
            compiler_params=pltpu.CompilerParams(
                collective_id=0, has_side_effects=True, vmem_limit_bytes=41943040
            ),
            name="fused",
        )(*[pltpu.with_memory_space_constraint(a, pltpu.HBM) for a in (span_ids, queries[0], keys[0], values[0], cotangent[0])])
        return attention[None], grad[None]

    return jax.shard_map(
        local,
        mesh=mesh,
        in_specs=(
            P("pipe", "ctx", "tp"),
            P("pipe", "ctx", "tp"),
            P("pipe", "ctx", "tp"),
            P("pipe", "ctx"),
            P("pipe", "ctx", None),
        ),
        out_specs=(P("pipe", "ctx", "tp"), P("pipe", "ctx", "tp")),
        check_vma=False,
    )
```

```python
import functools
import math

import jax
import jax.numpy as jnp
from jax import lax
from jax.experimental import pallas as pl
from jax.experimental.pallas import tpu as pltpu
from jax.sharding import PartitionSpec as P

HD = 128
PAD = 16
MESH = pl.DeviceIdType.MESH
BF = jnp.bfloat16
F32 = jnp.float32


class Spread:
    def __init__(self, n, long_right, ref_of, blocks, send, recv, at, straight=False):
        self.straight = straight
        self.n = n
        self.reach = n // 2 if long_right else (n - 1) // 2
        self.ref_of, self.blocks, self.send, self.recv, self.at = ref_of, blocks, send, recv, at

    def slots(self, group):
        rightward = [j for j in range(1, self.reach + 1) if min(j, 3) == group]
        leftward = [self.n - d for d in range(1, self.n - self.reach) if min(d, 3) == group]
        return rightward + leftward

    def emit(self, group):
        for j in self.slots(group):
            rightward = j <= self.reach
            apart = j if rightward else self.n - j
            via = 2 if apart > 2 else 0 if self.straight else apart - 1
            hop = apart - via
            signed = hop if rightward else -hop
            source = via if rightward else (self.n - via) % self.n
            pltpu.make_async_remote_copy(
                src_ref=self.ref_of(source, 0),
                dst_ref=self.ref_of(j, signed),
                send_sem=self.send,
                recv_sem=self.recv(group),
                device_id=self.at(signed),
                device_id_type=MESH,
            ).start()

    def begin(self):
        if self.straight:
            self.emit(2)
        self.emit(1)

    def take(self, group):
        count = len(self.slots(group))
        if count:
            settle(self.blocks(count), self.recv(group))
        return self.slots(group)

    def relay(self, group):
        slots = self.take(group)
        self.emit(group + 1)
        return slots


def settle(ref, sem):
    pltpu.make_async_copy(ref, ref, sem).wait()


def kernel(
    sizes, span_in, q, k, v, cot, att, grad,
    span, kbuf, vbuf, q4, scores, tops, probs, cbuf, cot_t, abuf, acc, out1, in1, out2, in2, last,
    sent, kv_recv, y_recv, a2a_recv, own_sem, x_recv, att_recv, in_sem, q_sem, att_sem, grad_sem, known,
):
    n_pipe, nz, nx = sizes
    p, c, t = lax.axis_index("pipe"), lax.axis_index("ctx"), lax.axis_index("tp")
    side = lax.rem(c, 2)
    z = lax.div(c, 2)
    tokens = q.shape[0]
    heads = q.shape[1] // HD
    span_len = tokens // 2
    feats = cot.shape[1] // nz
    chunk = tokens // nx
    half = feats // 2

    def at_z(d):
        return {"ctx": lax.rem(z + d + nz, nz) * 2 + side}

    def at_x(d):
        return {"tp": lax.rem(t + d + nx, nx)}

    across = c + 1 - 2 * side
    mirror = lax.rem(p + n_pipe // 2, n_pipe)
    y_peer = {"ctx": across}
    fold_peer = {"pipe": mirror, "ctx": across}
    pair_peer = {"pipe": mirror}

    barrier = pltpu.get_barrier_semaphore()
    beside = [at_z(d) for d in sorted({1, nz - 1})]
    peers = beside + [fold_peer, pair_peer]
    peers += [at_x(d) for d in sorted({hop % nx for hop in (-2, -1, 1, 2)} - {0})]
    for peer in peers:
        pl.semaphore_signal(barrier, inc=1, device_id=peer, device_id_type=MESH)

    span_load = pltpu.make_async_copy(span_in, span, in_sem.at[0])
    k_load = pltpu.make_async_copy(k, kbuf.at[0, 0:tokens], in_sem.at[1])
    v_load = pltpu.make_async_copy(v, vbuf.at[0], in_sem.at[2])
    q_load = [
        pltpu.make_async_copy(
            q.at[:, h * HD:(h + 1) * HD], q4.at[h * tokens:(h + 1) * tokens, :], q_sem)
        for h in range(heads)
    ]
    for copy in [span_load, k_load, v_load] + q_load:
        copy.start()
    span_load.wait()
    lane = lax.broadcasted_iota(jnp.int32, (PAD, HD), 1)
    id0, id1 = span[0, 0].astype(F32), span[0, 1].astype(F32)
    kbuf[0, tokens:, :] = jnp.where(lane < span_len, id0, id1).astype(BF)
    k_load.wait()
    v_load.wait()
    pl.semaphore_wait(barrier, len(peers))

    def tell(step, targets):
        for target in targets:
            pl.semaphore_signal(known.at[step], inc=1, device_id=target, device_id_type=MESH)

    tell(0, [pair_peer])
    rounds = min(nz // 2 - 1, 3)
    if rounds:
        tell(1, beside)

    def z_ring(buf, base, g, long_right):
        return Spread(
            nz, long_right, lambda j, way: buf.at[base + j], lambda count: buf.at[0:count],
            sent.at[g % 2], lambda group: kv_recv.at[g, group - 1], at_z,
        )

    k_own = z_ring(kbuf, 0, 0, True)
    v_own = z_ring(vbuf, 0, 1, False)
    k_far = z_ring(kbuf, nz, 2, False)
    v_far = z_ring(vbuf, nz, 3, True)
    k_over = pltpu.make_async_remote_copy(
        kbuf.at[0], kbuf.at[nz], sent.at[0], y_recv.at[0], device_id=y_peer, device_id_type=MESH)
    v_over = pltpu.make_async_remote_copy(
        vbuf.at[0], vbuf.at[nz], sent.at[1], y_recv.at[1], device_id=y_peer, device_id_type=MESH)
    k_own.begin()
    v_own.begin()
    pl.semaphore_wait(known.at[0], 1)
    k_over.start()
    v_over.start()

    rows = pl.ds(pl.multiple_of(t * chunk, chunk), chunk)

    def to_z(d):
        columns = pl.ds(pl.multiple_of(lax.rem(z + d, nz) * feats, feats), feats)
        return cot.at[rows, columns]

    own_cot = pltpu.make_async_copy(to_z(0), cbuf.at[t, 0], own_sem)
    own_cot.start()
    a2a = {
        d: pltpu.make_async_remote_copy(
            to_z(d), cbuf.at[t, d], sent.at[2], a2a_recv.at[d // (nz // 2)], device_id=at_z(d), device_id_type=MESH)
        for d in range(1, nz)
    }
    by_reach = {}
    for d in range(1, nz):
        by_reach.setdefault(min(d, nz - d), []).append(d)

    for d in by_reach[1]:
        a2a[d].start()

    def learn(step):
        if step <= rounds:
            pl.semaphore_wait(known.at[step], len(beside))
            if step < rounds:
                tell(step + 1, beside)
            for d in by_reach[step + 1]:
                a2a[d].start()

    row = lax.broadcasted_iota(jnp.int32, (tokens, HD), 0)
    col = lax.broadcasted_iota(jnp.int32, (tokens, HD), 1)
    query_pos = jnp.where(row < span_len, id0, id1) * span_len + lax.rem(row, span_len).astype(F32)
    key_off = lax.rem(col, span_len).astype(F32)

    settle(q4, q_sem)

    factor = math.log2(math.e) / math.sqrt(HD)

    def score(slot):
        keys = kbuf[slot, :tokens, :]
        ids = kbuf[slot, tokens:, :].astype(F32)
        key_pos = jnp.broadcast_to(ids[0:1, :], (tokens, HD)) * span_len + key_off
        bias = jnp.where(key_pos <= query_pos, 0.0, -1e30)
        for h in range(heads):
            part = lax.dot_general(
                q4[h * tokens:(h + 1) * tokens, :], keys, (((1,), (1,)), ((), ())), preferred_element_type=F32)
            part = part * factor + bias
            scores[h, slot] = part
            tops[h] = part if slot == 0 else jnp.maximum(tops[h], part)

    score(0)
    low, high = (0, nz // 2), (nz // 2, nz)

    def x_ring(part, long_right):
        def ref_of(j, way):
            place = lax.rem(t + way - j + 2 * nx, nx)
            return cbuf.at[place, part[0]:part[1]]

        return Spread(nx, long_right, ref_of, None, sent.at[3], lambda group: x_recv.at[group - 1], at_x, True)

    x_low, x_high = x_ring(low, True), x_ring(high, False)

    def x_take(group):
        count = len(x_low.slots(group)) + len(x_high.slots(group))
        if count:
            settle(cbuf.at[0:count // 2], x_recv.at[group - 1])

    learn(1)
    fresh = k_own.relay(1)
    v_own.relay(1)
    learn(2)
    k_over.wait_recv()
    k_far.begin()
    v_over.wait_recv()
    v_far.begin()
    learn(3)
    for slot in fresh + [nz]:
        score(slot)
    fresh = k_own.relay(2)
    v_own.relay(2)
    for slot in fresh:
        score(slot)
    fresh = k_far.relay(1)
    v_far.relay(1)
    for slot in fresh:
        score(nz + slot)
    fresh = k_far.relay(2)
    v_far.relay(2)
    own_cot.wait()
    settle(cbuf.at[t, 1:nz // 2], a2a_recv.at[0])
    x_low.begin()
    settle(cbuf.at[t, nz // 2:nz], a2a_recv.at[1])
    x_high.begin()
    for slot in fresh:
        score(nz + slot)
    for slot in k_own.take(3):
        score(slot)
    for slot in k_far.take(3):
        score(nz + slot)

    a_rings = [
        Spread(
            nz, h % 2 == 0, functools.partial(lambda h, j, way: abuf.at[h, j], h),
            functools.partial(lambda h, count: abuf.at[h, 0:count], h), sent.at[4],
            functools.partial(lambda h, group: att_recv.at[h, group - 1], h), at_z)
        for h in range(heads)
    ]

    def attend(h):
        top = jnp.broadcast_to(jnp.max(tops[h], axis=-1, keepdims=True), (tokens, HD))
        total = jnp.zeros((tokens, HD), F32)
        for slot in range(2 * nz):
            weights = jnp.exp2(scores[h, slot] - top)
            total = total + weights
            probs[:, slot * HD:(slot + 1) * HD] = weights.astype(BF)
        if h == 0:
            v_own.take(3)
            v_far.take(3)
        mixed = jnp.dot(probs[...], vbuf[...].reshape(2 * nz * tokens, HD), preferred_element_type=F32)
        out = (mixed / jnp.sum(total, axis=-1, keepdims=True)).astype(BF)
        abuf[h, 0] = out

    att_out = [
        pltpu.make_async_copy(abuf.at[h, 0], att.at[:, h * HD:(h + 1) * HD], att_sem) for h in range(heads)
    ]
    for h in range(heads):
        attend(h)
        a_rings[h].begin()
    for copy in att_out:
        copy.start()

    def turn(j):
        block = cbuf[:, j].reshape(tokens, feats)
        cot_t[:, j * tokens:(j + 1) * tokens] = block.T

    for h in range(heads):
        a_rings[h].relay(1)
    x_take(2)
    x_low.emit(3)
    x_high.emit(3)
    for h in range(heads):
        a_rings[h].relay(2)
    x_take(1)
    x_take(3)
    for j in range(nz):
        turn(j)

    fold = [
        pltpu.make_async_remote_copy(
            out1.at[h, 1 - side], in1.at[h], sent.at[5], y_recv.at[2 + h],
            device_id=fold_peer, device_id_type=MESH)
        for h in range(heads)
    ]
    pair = [
        pltpu.make_async_remote_copy(
            out2.at[h], in2.at[h], sent.at[6], y_recv.at[2 + heads + h],
            device_id=pair_peer, device_id_type=MESH)
        for h in range(heads)
    ]
    for h in range(heads):
        a_rings[h].take(3)
        summed = jnp.dot(cot_t[...], abuf[h].reshape(nz * tokens, HD), preferred_element_type=F32)
        acc[h] = summed.reshape(2, half, HD)
        out1[h] = summed.astype(BF).reshape(2, half, HD)
        fold[h].start()
    for h in range(heads):
        fold[h].wait_recv()
        both = acc[h, side] + in1[h].astype(F32)
        acc[h, side] = both
        out2[h] = both.astype(BF)
        pair[h].start()
    grad_out = [
        pltpu.make_async_copy(last.at[h], grad.at[:, h * HD:(h + 1) * HD], grad_sem) for h in range(heads)
    ]
    for h in range(heads):
        pair[h].wait_recv()
        last[h] = (acc[h, side] + in2[h].astype(F32)).astype(BF)
        grad_out[h].start()

    for g, ref in enumerate(
        [kbuf.at[1:2 * nz], vbuf.at[1:2 * nz], cbuf.at[0, 1:nz], cbuf.at[0:nx - 1], abuf.at[:, 1:nz], in1, in2]
    ):
        settle(ref, sent.at[g])
    settle(att, att_sem)
    settle(grad, grad_sem)


def solution(mesh):
    n_pipe, n_ctx, nx = mesh.shape["pipe"], mesh.shape["ctx"], mesh.shape["tp"]
    nz = n_ctx // 2

    def local(queries, keys, values, span_ids, cotangent):
        tokens, width = queries.shape[1:]
        heads = width // HD
        feats = cotangent.shape[2] // nz
        half = feats // 2
        dma = pltpu.SemaphoreType.DMA
        hbm = pl.BlockSpec(memory_space=pltpu.HBM)
        attention, grad = pl.pallas_call(
            functools.partial(kernel, (n_pipe, nz, nx)),
            out_shape=(
                jax.ShapeDtypeStruct((tokens, width), BF),
                jax.ShapeDtypeStruct((half, width), BF),
            ),
            in_specs=[hbm] * 5,
            out_specs=(hbm, hbm),
            scratch_shapes=[
                pltpu.SMEM((1, 2), jnp.int32),
                pltpu.VMEM((2 * nz, tokens + PAD, HD), BF),
                pltpu.VMEM((2 * nz, tokens, HD), BF),
                pltpu.VMEM((heads * tokens, HD), BF),
                pltpu.VMEM((heads, 2 * nz, tokens, HD), F32),
                pltpu.VMEM((heads, tokens, HD), F32),
                pltpu.VMEM((tokens, 2 * nz * HD), BF),
                pltpu.VMEM((nx, nz, tokens // nx, feats), BF),
                pltpu.VMEM((feats, nz * tokens), BF),
                pltpu.VMEM((heads, nz, tokens, HD), BF),
                pltpu.VMEM((heads, 2, half, HD), F32),
                pltpu.VMEM((heads, 2, half, HD), BF),
                pltpu.VMEM((heads, half, HD), BF),
                pltpu.VMEM((heads, half, HD), BF),
                pltpu.VMEM((heads, half, HD), BF),
                pltpu.VMEM((heads, half, HD), BF),
                dma((7,)),
                dma((4, 3)),
                dma((2 + 2 * heads,)),
                dma((2,)),
                dma,
                dma((3,)),
                dma((heads, 3)),
                dma((3,)),
                dma,
                dma,
                dma,
                pltpu.SemaphoreType.REGULAR((nz // 2,)),
            ],
            compiler_params=pltpu.CompilerParams(
                collective_id=0, has_side_effects=True, vmem_limit_bytes=41943040
            ),
            name="fused",
        )(*[pltpu.with_memory_space_constraint(a, pltpu.HBM) for a in (span_ids, queries[0], keys[0], values[0], cotangent[0])])
        return attention[None], grad[None]

    return jax.shard_map(
        local,
        mesh=mesh,
        in_specs=(
            P("pipe", "ctx", "tp"),
            P("pipe", "ctx", "tp"),
            P("pipe", "ctx", "tp"),
            P("pipe", "ctx"),
            P("pipe", "ctx", None),
        ),
        out_specs=(P("pipe", "ctx", "tp"), P("pipe", "ctx", "tp")),
        check_vma=False,
    )
```

```python
import functools
import math

import jax
import jax.numpy as jnp
from jax import lax
from jax.experimental import pallas as pl
from jax.experimental.pallas import tpu as pltpu
from jax.sharding import PartitionSpec as P

HD = 128
PAD = 16
MESH = pl.DeviceIdType.MESH
BF = jnp.bfloat16
F32 = jnp.float32


class Spread:
    def __init__(self, n, long_right, ref_of, blocks, send, recv, at, straight=False):
        self.straight = straight
        self.n = n
        self.reach = n // 2 if long_right else (n - 1) // 2
        self.ref_of, self.blocks, self.send, self.recv, self.at = ref_of, blocks, send, recv, at

    def slots(self, group):
        rightward = [j for j in range(1, self.reach + 1) if min(j, 3) == group]
        leftward = [self.n - d for d in range(1, self.n - self.reach) if min(d, 3) == group]
        return rightward + leftward

    def emit(self, group):
        for j in self.slots(group):
            rightward = j <= self.reach
            apart = j if rightward else self.n - j
            via = 2 if apart > 2 else 0 if self.straight else apart - 1
            hop = apart - via
            signed = hop if rightward else -hop
            source = via if rightward else (self.n - via) % self.n
            pltpu.make_async_remote_copy(
                src_ref=self.ref_of(source, 0),
                dst_ref=self.ref_of(j, signed),
                send_sem=self.send,
                recv_sem=self.recv(group),
                device_id=self.at(signed),
                device_id_type=MESH,
            ).start()

    def begin(self):
        if self.straight:
            self.emit(2)
        self.emit(1)

    def take(self, group):
        count = len(self.slots(group))
        if count:
            settle(self.blocks(count), self.recv(group))
        return self.slots(group)

    def relay(self, group):
        slots = self.take(group)
        self.emit(group + 1)
        return slots


def settle(ref, sem):
    pltpu.make_async_copy(ref, ref, sem).wait()


def kernel(
    sizes, span_in, q, k, v, cot, att, grad,
    span, kbuf, vbuf, q4, scores, tops, probs, cbuf, cot_t, abuf, acc, out1, in1, out2, in2, last,
    sent, kv_recv, y_recv, a2a_recv, own_sem, x_recv, att_recv, in_sem, q_sem, att_sem, grad_sem, known,
):
    n_pipe, nz, nx = sizes
    p, c, t = lax.axis_index("pipe"), lax.axis_index("ctx"), lax.axis_index("tp")
    side = lax.rem(c, 2)
    z = lax.div(c, 2)
    tokens = q.shape[0]
    heads = q.shape[1] // HD
    span_len = tokens // 2
    feats = cot.shape[1] // nz
    chunk = tokens // nx
    half = feats // 2

    def at_z(d):
        return {"ctx": lax.rem(z + d + nz, nz) * 2 + side}

    def at_x(d):
        return {"tp": lax.rem(t + d + nx, nx)}

    across = c + 1 - 2 * side
    mirror = lax.rem(p + n_pipe // 2, n_pipe)
    y_peer = {"ctx": across}
    fold_peer = {"pipe": mirror, "ctx": across}
    pair_peer = {"pipe": mirror}

    barrier = pltpu.get_barrier_semaphore()
    beside = [at_z(d) for d in sorted({1, nz - 1})]
    peers = beside + [fold_peer, pair_peer]
    peers += [at_x(d) for d in sorted({hop % nx for hop in (-2, -1, 1, 2)} - {0})]
    for peer in peers:
        pl.semaphore_signal(barrier, inc=1, device_id=peer, device_id_type=MESH)

    span_load = pltpu.make_async_copy(span_in, span, in_sem.at[0])
    k_load = pltpu.make_async_copy(k, kbuf.at[0, 0:tokens], in_sem.at[1])
    v_load = pltpu.make_async_copy(v, vbuf.at[0], in_sem.at[2])
    q_load = [
        pltpu.make_async_copy(
            q.at[:, h * HD:(h + 1) * HD], q4.at[h * tokens:(h + 1) * tokens, :], q_sem)
        for h in range(heads)
    ]
    for copy in [span_load, k_load, v_load] + q_load:
        copy.start()
    span_load.wait()
    lane = lax.broadcasted_iota(jnp.int32, (PAD, HD), 1)
    id0, id1 = span[0, 0].astype(F32), span[0, 1].astype(F32)
    kbuf[0, tokens:, :] = jnp.where(lane < span_len, id0, id1).astype(BF)
    k_load.wait()
    v_load.wait()
    pl.semaphore_wait(barrier, len(peers))

    def tell(step, targets):
        for target in targets:
            pl.semaphore_signal(known.at[step], inc=1, device_id=target, device_id_type=MESH)

    tell(0, [pair_peer])
    rounds = min(nz // 2 - 1, 3)
    if rounds:
        tell(1, beside)

    def z_ring(buf, base, g, long_right):
        return Spread(
            nz, long_right, lambda j, way: buf.at[base + j], lambda count: buf.at[0:count],
            sent.at[g % 2], lambda group: kv_recv.at[g, group - 1], at_z,
        )

    k_own = z_ring(kbuf, 0, 0, True)
    v_own = z_ring(vbuf, 0, 1, False)
    k_far = z_ring(kbuf, nz, 2, False)
    v_far = z_ring(vbuf, nz, 3, True)
    k_over = pltpu.make_async_remote_copy(
        kbuf.at[0], kbuf.at[nz], sent.at[0], y_recv.at[0], device_id=y_peer, device_id_type=MESH)
    v_over = pltpu.make_async_remote_copy(
        vbuf.at[0], vbuf.at[nz], sent.at[1], y_recv.at[1], device_id=y_peer, device_id_type=MESH)
    k_own.begin()
    v_own.begin()
    pl.semaphore_wait(known.at[0], 1)
    k_over.start()
    v_over.start()

    rows = pl.ds(pl.multiple_of(t * chunk, chunk), chunk)

    def to_z(d):
        columns = pl.ds(pl.multiple_of(lax.rem(z + d, nz) * feats, feats), feats)
        return cot.at[rows, columns]

    own_cot = pltpu.make_async_copy(to_z(0), cbuf.at[t, 0], own_sem)
    own_cot.start()
    a2a = {
        d: pltpu.make_async_remote_copy(
            to_z(d), cbuf.at[t, d], sent.at[2], a2a_recv.at[d // (nz // 2)], device_id=at_z(d), device_id_type=MESH)
        for d in range(1, nz)
    }
    by_reach = {}
    for d in range(1, nz):
        by_reach.setdefault(min(d, nz - d), []).append(d)

    for d in by_reach[1]:
        a2a[d].start()

    def learn(step):
        if step <= rounds:
            pl.semaphore_wait(known.at[step], len(beside))
            if step < rounds:
                tell(step + 1, beside)
            for d in by_reach[step + 1]:
                a2a[d].start()

    row = lax.broadcasted_iota(jnp.int32, (tokens, HD), 0)
    col = lax.broadcasted_iota(jnp.int32, (tokens, HD), 1)
    query_pos = jnp.where(row < span_len, id0, id1) * span_len + lax.rem(row, span_len).astype(F32)
    key_off = lax.rem(col, span_len).astype(F32)

    settle(q4, q_sem)

    factor = math.log2(math.e) / math.sqrt(HD)

    def score(slot):
        keys = kbuf[slot, :tokens, :]
        ids = kbuf[slot, tokens:, :].astype(F32)
        key_pos = jnp.broadcast_to(ids[0:1, :], (tokens, HD)) * span_len + key_off
        bias = jnp.where(key_pos <= query_pos, 0.0, -1e30)
        for h in range(heads):
            part = lax.dot_general(
                q4[h * tokens:(h + 1) * tokens, :], keys, (((1,), (1,)), ((), ())), preferred_element_type=F32)
            part = part * factor + bias
            scores[h, slot] = part
            tops[h] = part if slot == 0 else jnp.maximum(tops[h], part)

    score(0)
    low, high = (0, nz // 2), (nz // 2, nz)

    def x_ring(part, long_right):
        def ref_of(j, way):
            place = lax.rem(t + way - j + 2 * nx, nx)
            return cbuf.at[place, part[0]:part[1]]

        return Spread(nx, long_right, ref_of, None, sent.at[3], lambda group: x_recv.at[group - 1], at_x, True)

    x_low, x_high = x_ring(low, True), x_ring(high, False)

    def x_take(group):
        count = len(x_low.slots(group)) + len(x_high.slots(group))
        if count:
            settle(cbuf.at[0:count // 2], x_recv.at[group - 1])

    learn(1)
    fresh = k_own.relay(1)
    v_own.relay(1)
    learn(2)
    k_over.wait_recv()
    k_far.begin()
    v_over.wait_recv()
    v_far.begin()
    learn(3)
    for slot in fresh + [nz]:
        score(slot)
    fresh = k_own.relay(2)
    v_own.relay(2)
    for slot in fresh:
        score(slot)
    fresh = k_far.relay(1)
    v_far.relay(1)
    for slot in fresh:
        score(nz + slot)
    own_cot.wait()
    settle(cbuf.at[t, 1:nz // 2], a2a_recv.at[0])
    x_low.begin()
    fresh = k_far.relay(2)
    settle(cbuf.at[t, nz // 2:nz], a2a_recv.at[1])
    x_high.begin()
    v_far.relay(2)
    for slot in fresh:
        score(nz + slot)
    for slot in k_own.take(3):
        score(slot)
    for slot in k_far.take(3):
        score(nz + slot)

    a_rings = [
        Spread(
            nz, h % 2 == 0, functools.partial(lambda h, j, way: abuf.at[h, j], h),
            functools.partial(lambda h, count: abuf.at[h, 0:count], h), sent.at[4],
            functools.partial(lambda h, group: att_recv.at[h, group - 1], h), at_z)
        for h in range(heads)
    ]

    def attend(h):
        top = jnp.broadcast_to(jnp.max(tops[h], axis=-1, keepdims=True), (tokens, HD))
        total = jnp.zeros((tokens, HD), F32)
        for slot in range(2 * nz):
            weights = jnp.exp2(scores[h, slot] - top)
            total = total + weights
            probs[:, slot * HD:(slot + 1) * HD] = weights.astype(BF)
        if h == 0:
            v_own.take(3)
            v_far.take(3)
        mixed = jnp.dot(probs[...], vbuf[...].reshape(2 * nz * tokens, HD), preferred_element_type=F32)
        out = (mixed / jnp.sum(total, axis=-1, keepdims=True)).astype(BF)
        abuf[h, 0] = out

    att_out = [
        pltpu.make_async_copy(abuf.at[h, 0], att.at[:, h * HD:(h + 1) * HD], att_sem) for h in range(heads)
    ]
    for h in range(heads):
        attend(h)
        a_rings[h].begin()
    x_take(2)
    x_low.emit(3)
    x_high.emit(3)
    for copy in att_out:
        copy.start()

    def turn(j):
        block = cbuf[:, j].reshape(tokens, feats)
        cot_t[:, j * tokens:(j + 1) * tokens] = block.T

    for h in range(heads):
        a_rings[h].relay(1)
    for h in range(heads):
        a_rings[h].relay(2)
    x_take(1)
    x_take(3)
    for j in range(nz):
        turn(j)

    fold = [
        pltpu.make_async_remote_copy(
            out1.at[h, 1 - side], in1.at[h], sent.at[5], y_recv.at[2 + h],
            device_id=fold_peer, device_id_type=MESH)
        for h in range(heads)
    ]
    pair = [
        pltpu.make_async_remote_copy(
            out2.at[h], in2.at[h], sent.at[6], y_recv.at[2 + heads + h],
            device_id=pair_peer, device_id_type=MESH)
        for h in range(heads)
    ]
    for h in range(heads):
        a_rings[h].take(3)
        summed = jnp.dot(cot_t[...], abuf[h].reshape(nz * tokens, HD), preferred_element_type=F32)
        acc[h] = summed.reshape(2, half, HD)
        out1[h] = summed.astype(BF).reshape(2, half, HD)
        fold[h].start()
    for h in range(heads):
        fold[h].wait_recv()
        both = acc[h, side] + in1[h].astype(F32)
        acc[h, side] = both
        out2[h] = both.astype(BF)
        pair[h].start()
    grad_out = [
        pltpu.make_async_copy(last.at[h], grad.at[:, h * HD:(h + 1) * HD], grad_sem) for h in range(heads)
    ]
    for h in range(heads):
        pair[h].wait_recv()
        last[h] = (acc[h, side] + in2[h].astype(F32)).astype(BF)
        grad_out[h].start()

    for g, ref in enumerate(
        [kbuf.at[1:2 * nz], vbuf.at[1:2 * nz], cbuf.at[0, 1:nz], cbuf.at[0:nx - 1], abuf.at[:, 1:nz], in1, in2]
    ):
        settle(ref, sent.at[g])
    settle(att, att_sem)
    settle(grad, grad_sem)


def solution(mesh):
    n_pipe, n_ctx, nx = mesh.shape["pipe"], mesh.shape["ctx"], mesh.shape["tp"]
    nz = n_ctx // 2

    def local(queries, keys, values, span_ids, cotangent):
        tokens, width = queries.shape[1:]
        heads = width // HD
        feats = cotangent.shape[2] // nz
        half = feats // 2
        dma = pltpu.SemaphoreType.DMA
        hbm = pl.BlockSpec(memory_space=pltpu.HBM)
        attention, grad = pl.pallas_call(
            functools.partial(kernel, (n_pipe, nz, nx)),
            out_shape=(
                jax.ShapeDtypeStruct((tokens, width), BF),
                jax.ShapeDtypeStruct((half, width), BF),
            ),
            in_specs=[hbm] * 5,
            out_specs=(hbm, hbm),
            scratch_shapes=[
                pltpu.SMEM((1, 2), jnp.int32),
                pltpu.VMEM((2 * nz, tokens + PAD, HD), BF),
                pltpu.VMEM((2 * nz, tokens, HD), BF),
                pltpu.VMEM((heads * tokens, HD), BF),
                pltpu.VMEM((heads, 2 * nz, tokens, HD), F32),
                pltpu.VMEM((heads, tokens, HD), F32),
                pltpu.VMEM((tokens, 2 * nz * HD), BF),
                pltpu.VMEM((nx, nz, tokens // nx, feats), BF),
                pltpu.VMEM((feats, nz * tokens), BF),
                pltpu.VMEM((heads, nz, tokens, HD), BF),
                pltpu.VMEM((heads, 2, half, HD), F32),
                pltpu.VMEM((heads, 2, half, HD), BF),
                pltpu.VMEM((heads, half, HD), BF),
                pltpu.VMEM((heads, half, HD), BF),
                pltpu.VMEM((heads, half, HD), BF),
                pltpu.VMEM((heads, half, HD), BF),
                dma((7,)),
                dma((4, 3)),
                dma((2 + 2 * heads,)),
                dma((2,)),
                dma,
                dma((3,)),
                dma((heads, 3)),
                dma((3,)),
                dma,
                dma,
                dma,
                pltpu.SemaphoreType.REGULAR((nz // 2,)),
            ],
            compiler_params=pltpu.CompilerParams(
                collective_id=0, has_side_effects=True, vmem_limit_bytes=41943040
            ),
            name="fused",
        )(*[pltpu.with_memory_space_constraint(a, pltpu.HBM) for a in (span_ids, queries[0], keys[0], values[0], cotangent[0])])
        return attention[None], grad[None]

    return jax.shard_map(
        local,
        mesh=mesh,
        in_specs=(
            P("pipe", "ctx", "tp"),
            P("pipe", "ctx", "tp"),
            P("pipe", "ctx", "tp"),
            P("pipe", "ctx"),
            P("pipe", "ctx", None),
        ),
        out_specs=(P("pipe", "ctx", "tp"), P("pipe", "ctx", "tp")),
        check_vma=False,
    )
```

```python
import functools
import math

import jax
import jax.numpy as jnp
from jax import lax
from jax.experimental import pallas as pl
from jax.experimental.pallas import tpu as pltpu
from jax.sharding import PartitionSpec as P

HD = 128
PAD = 16
MESH = pl.DeviceIdType.MESH
BF = jnp.bfloat16
F32 = jnp.float32


class Spread:
    def __init__(self, n, long_right, ref_of, blocks, send, recv, at, straight=False):
        self.straight = straight
        self.n = n
        self.reach = n // 2 if long_right else (n - 1) // 2
        self.ref_of, self.blocks, self.send, self.recv, self.at = ref_of, blocks, send, recv, at

    def slots(self, group):
        rightward = [j for j in range(1, self.reach + 1) if min(j, 3) == group]
        leftward = [self.n - d for d in range(1, self.n - self.reach) if min(d, 3) == group]
        return rightward + leftward

    def emit(self, group):
        for j in self.slots(group):
            rightward = j <= self.reach
            apart = j if rightward else self.n - j
            via = 2 if apart > 2 else 0 if self.straight else apart - 1
            hop = apart - via
            signed = hop if rightward else -hop
            source = via if rightward else (self.n - via) % self.n
            pltpu.make_async_remote_copy(
                src_ref=self.ref_of(source, 0),
                dst_ref=self.ref_of(j, signed),
                send_sem=self.send,
                recv_sem=self.recv(group),
                device_id=self.at(signed),
                device_id_type=MESH,
            ).start()

    def begin(self):
        if self.straight:
            self.emit(2)
        self.emit(1)

    def take(self, group):
        count = len(self.slots(group))
        if count:
            settle(self.blocks(count), self.recv(group))
        return self.slots(group)

    def relay(self, group):
        slots = self.take(group)
        self.emit(group + 1)
        return slots


def settle(ref, sem):
    pltpu.make_async_copy(ref, ref, sem).wait()


def kernel(
    sizes, span_in, q, k, v, cot, att, grad,
    span, kbuf, vbuf, q4, scores, tops, probs, cbuf, cot_t, abuf, acc, out1, in1, out2, in2, last,
    sent, kv_recv, y_recv, a2a_recv, own_sem, x_recv, att_recv, in_sem, q_sem, att_sem, grad_sem, known,
):
    n_pipe, nz, nx = sizes
    p, c, t = lax.axis_index("pipe"), lax.axis_index("ctx"), lax.axis_index("tp")
    side = lax.rem(c, 2)
    z = lax.div(c, 2)
    tokens = q.shape[0]
    heads = q.shape[1] // HD
    span_len = tokens // 2
    feats = cot.shape[1] // nz
    chunk = tokens // nx
    half = feats // 2

    def at_z(d):
        return {"ctx": lax.rem(z + d + nz, nz) * 2 + side}

    def at_x(d):
        return {"tp": lax.rem(t + d + nx, nx)}

    across = c + 1 - 2 * side
    mirror = lax.rem(p + n_pipe // 2, n_pipe)
    y_peer = {"ctx": across}
    fold_peer = {"pipe": mirror, "ctx": across}
    pair_peer = {"pipe": mirror}

    barrier = pltpu.get_barrier_semaphore()
    beside = [at_z(d) for d in sorted({1, nz - 1})]
    peers = beside + [fold_peer, pair_peer]
    peers += [at_x(d) for d in sorted({hop % nx for hop in (-2, -1, 1, 2)} - {0})]
    for peer in peers:
        pl.semaphore_signal(barrier, inc=1, device_id=peer, device_id_type=MESH)

    span_load = pltpu.make_async_copy(span_in, span, in_sem.at[0])
    k_load = pltpu.make_async_copy(k, kbuf.at[0, 0:tokens], in_sem.at[1])
    v_load = pltpu.make_async_copy(v, vbuf.at[0], in_sem.at[2])
    q_load = [
        pltpu.make_async_copy(
            q.at[:, h * HD:(h + 1) * HD], q4.at[h * tokens:(h + 1) * tokens, :], q_sem)
        for h in range(heads)
    ]
    for copy in [span_load, k_load, v_load] + q_load:
        copy.start()
    span_load.wait()
    lane = lax.broadcasted_iota(jnp.int32, (PAD, HD), 1)
    id0, id1 = span[0, 0].astype(F32), span[0, 1].astype(F32)
    kbuf[0, tokens:, :] = jnp.where(lane < span_len, id0, id1).astype(BF)
    k_load.wait()
    v_load.wait()
    pl.semaphore_wait(barrier, len(peers))

    def tell(step, targets):
        for target in targets:
            pl.semaphore_signal(known.at[step], inc=1, device_id=target, device_id_type=MESH)

    tell(0, [pair_peer])
    rounds = min(nz // 2 - 1, 3)
    if rounds:
        tell(1, beside)

    def z_ring(buf, base, g, long_right):
        return Spread(
            nz, long_right, lambda j, way: buf.at[base + j], lambda count: buf.at[0:count],
            sent.at[g % 2], lambda group: kv_recv.at[g, group - 1], at_z,
        )

    k_own = z_ring(kbuf, 0, 0, True)
    v_own = z_ring(vbuf, 0, 1, False)
    k_far = z_ring(kbuf, nz, 2, False)
    v_far = z_ring(vbuf, nz, 3, True)
    k_over = pltpu.make_async_remote_copy(
        kbuf.at[0], kbuf.at[nz], sent.at[0], y_recv.at[0], device_id=y_peer, device_id_type=MESH)
    v_over = pltpu.make_async_remote_copy(
        vbuf.at[0], vbuf.at[nz], sent.at[1], y_recv.at[1], device_id=y_peer, device_id_type=MESH)
    k_own.begin()
    v_own.begin()
    pl.semaphore_wait(known.at[0], 1)
    k_over.start()
    v_over.start()

    rows = pl.ds(pl.multiple_of(t * chunk, chunk), chunk)

    def to_z(d):
        columns = pl.ds(pl.multiple_of(lax.rem(z + d, nz) * feats, feats), feats)
        return cot.at[rows, columns]

    own_cot = pltpu.make_async_copy(to_z(0), cbuf.at[t, 0], own_sem)
    own_cot.start()
    a2a = {
        d: pltpu.make_async_remote_copy(
            to_z(d), cbuf.at[t, d], sent.at[2], a2a_recv.at[d // (nz // 2)], device_id=at_z(d), device_id_type=MESH)
        for d in range(1, nz)
    }
    by_reach = {}
    for d in range(1, nz):
        by_reach.setdefault(min(d, nz - d), []).append(d)

    for d in by_reach[1]:
        a2a[d].start()

    def learn(step):
        if step <= rounds:
            pl.semaphore_wait(known.at[step], len(beside))
            if step < rounds:
                tell(step + 1, beside)
            for d in by_reach[step + 1]:
                a2a[d].start()

    row = lax.broadcasted_iota(jnp.int32, (tokens, HD), 0)
    col = lax.broadcasted_iota(jnp.int32, (tokens, HD), 1)
    query_pos = jnp.where(row < span_len, id0, id1) * span_len + lax.rem(row, span_len).astype(F32)
    key_off = lax.rem(col, span_len).astype(F32)

    settle(q4, q_sem)

    factor = math.log2(math.e) / math.sqrt(HD)

    def score(slot):
        keys = kbuf[slot, :tokens, :]
        ids = kbuf[slot, tokens:, :].astype(F32)
        key_pos = jnp.broadcast_to(ids[0:1, :], (tokens, HD)) * span_len + key_off
        bias = jnp.where(key_pos <= query_pos, 0.0, -1e30)
        for h in range(heads):
            part = lax.dot_general(
                q4[h * tokens:(h + 1) * tokens, :], keys, (((1,), (1,)), ((), ())), preferred_element_type=F32)
            part = part * factor + bias
            scores[h, slot] = part
            tops[h] = part if slot == 0 else jnp.maximum(tops[h], part)

    score(0)
    low, high = (0, nz // 2), (nz // 2, nz)

    def x_ring(part, long_right):
        def ref_of(j, way):
            place = lax.rem(t + way - j + 2 * nx, nx)
            return cbuf.at[place, part[0]:part[1]]

        return Spread(nx, long_right, ref_of, None, sent.at[3], lambda group: x_recv.at[group - 1], at_x, True)

    x_low, x_high = x_ring(low, True), x_ring(high, False)

    def x_take(group):
        count = len(x_low.slots(group)) + len(x_high.slots(group))
        if count:
            settle(cbuf.at[0:count // 2], x_recv.at[group - 1])

    learn(1)
    fresh = k_own.relay(1)
    v_own.relay(1)
    learn(2)
    k_over.wait_recv()
    k_far.begin()
    v_over.wait_recv()
    v_far.begin()
    learn(3)
    for slot in fresh + [nz]:
        score(slot)
    fresh = k_own.relay(2)
    v_own.relay(2)
    for slot in fresh:
        score(slot)
    fresh = k_far.relay(1)
    v_far.relay(1)
    for slot in fresh:
        score(nz + slot)
    own_cot.wait()
    settle(cbuf.at[t, 1:nz // 2], a2a_recv.at[0])
    x_low.begin()
    fresh = k_far.relay(2)
    settle(cbuf.at[t, nz // 2:nz], a2a_recv.at[1])
    x_high.begin()
    v_far.relay(2)
    for slot in fresh:
        score(nz + slot)
    for slot in k_own.take(3):
        score(slot)
    for slot in k_far.take(3):
        score(nz + slot)

    a_rings = [
        Spread(
            nz, h % 2 == 0, functools.partial(lambda h, j, way: abuf.at[h, j], h),
            functools.partial(lambda h, count: abuf.at[h, 0:count], h), sent.at[4],
            functools.partial(lambda h, group: att_recv.at[h, group - 1], h), at_z)
        for h in range(heads)
    ]

    def attend(h):
        top = jnp.broadcast_to(jnp.max(tops[h], axis=-1, keepdims=True), (tokens, HD))
        total = jnp.zeros((tokens, HD), F32)
        for slot in range(2 * nz):
            weights = jnp.exp2(scores[h, slot] - top)
            total = total + weights
            probs[:, slot * HD:(slot + 1) * HD] = weights.astype(BF)
        if h == 0:
            v_own.take(3)
            v_far.take(3)
        mixed = jnp.dot(probs[...], vbuf[...].reshape(2 * nz * tokens, HD), preferred_element_type=F32)
        out = (mixed / jnp.sum(total, axis=-1, keepdims=True)).astype(BF)
        abuf[h, 0] = out

    att_out = [
        pltpu.make_async_copy(abuf.at[h, 0], att.at[:, h * HD:(h + 1) * HD], att_sem) for h in range(heads)
    ]
    for h in range(heads):
        attend(h)
        a_rings[h].begin()
    x_take(2)
    x_low.emit(3)
    x_high.emit(3)
    for copy in att_out:
        copy.start()

    def turn(j):
        block = cbuf[:, j].reshape(tokens, feats)
        cot_t[:, j * tokens:(j + 1) * tokens] = block.T

    for h in range(heads):
        a_rings[h].relay(1)
    for h in range(heads):
        a_rings[h].relay(2)
    x_take(1)
    x_take(3)
    for j in range(nz):
        turn(j)

    fold = [
        pltpu.make_async_remote_copy(
            out1.at[h, 1 - side], in1.at[h], sent.at[5], y_recv.at[2 + h],
            device_id=fold_peer, device_id_type=MESH)
        for h in range(heads)
    ]
    pair = [
        pltpu.make_async_remote_copy(
            out2.at[h], in2.at[h], sent.at[6], y_recv.at[2 + heads + h],
            device_id=pair_peer, device_id_type=MESH)
        for h in range(heads)
    ]

    def product(h, part):
        features = cot_t[pl.ds(pl.multiple_of(part * half, half), half), :]
        return jnp.dot(features, abuf[h].reshape(nz * tokens, HD), preferred_element_type=F32)

    for h in range(heads):
        a_rings[h].take(3)
        out1[h, 1 - side] = product(h, 1 - side).astype(BF)
        fold[h].start()
    for h in range(heads):
        acc[h, side] = product(h, side)
    for h in range(heads):
        fold[h].wait_recv()
        both = acc[h, side] + in1[h].astype(F32)
        acc[h, side] = both
        out2[h] = both.astype(BF)
        pair[h].start()
    grad_out = [
        pltpu.make_async_copy(last.at[h], grad.at[:, h * HD:(h + 1) * HD], grad_sem) for h in range(heads)
    ]
    for h in range(heads):
        pair[h].wait_recv()
        last[h] = (acc[h, side] + in2[h].astype(F32)).astype(BF)
        grad_out[h].start()

    for g, ref in enumerate(
        [kbuf.at[1:2 * nz], vbuf.at[1:2 * nz], cbuf.at[0, 1:nz], cbuf.at[0:nx - 1], abuf.at[:, 1:nz], in1, in2]
    ):
        settle(ref, sent.at[g])
    settle(att, att_sem)
    settle(grad, grad_sem)


def solution(mesh):
    n_pipe, n_ctx, nx = mesh.shape["pipe"], mesh.shape["ctx"], mesh.shape["tp"]
    nz = n_ctx // 2

    def local(queries, keys, values, span_ids, cotangent):
        tokens, width = queries.shape[1:]
        heads = width // HD
        feats = cotangent.shape[2] // nz
        half = feats // 2
        dma = pltpu.SemaphoreType.DMA
        hbm = pl.BlockSpec(memory_space=pltpu.HBM)
        attention, grad = pl.pallas_call(
            functools.partial(kernel, (n_pipe, nz, nx)),
            out_shape=(
                jax.ShapeDtypeStruct((tokens, width), BF),
                jax.ShapeDtypeStruct((half, width), BF),
            ),
            in_specs=[hbm] * 5,
            out_specs=(hbm, hbm),
            scratch_shapes=[
                pltpu.SMEM((1, 2), jnp.int32),
                pltpu.VMEM((2 * nz, tokens + PAD, HD), BF),
                pltpu.VMEM((2 * nz, tokens, HD), BF),
                pltpu.VMEM((heads * tokens, HD), BF),
                pltpu.VMEM((heads, 2 * nz, tokens, HD), F32),
                pltpu.VMEM((heads, tokens, HD), F32),
                pltpu.VMEM((tokens, 2 * nz * HD), BF),
                pltpu.VMEM((nx, nz, tokens // nx, feats), BF),
                pltpu.VMEM((feats, nz * tokens), BF),
                pltpu.VMEM((heads, nz, tokens, HD), BF),
                pltpu.VMEM((heads, 2, half, HD), F32),
                pltpu.VMEM((heads, 2, half, HD), BF),
                pltpu.VMEM((heads, half, HD), BF),
                pltpu.VMEM((heads, half, HD), BF),
                pltpu.VMEM((heads, half, HD), BF),
                pltpu.VMEM((heads, half, HD), BF),
                dma((7,)),
                dma((4, 3)),
                dma((2 + 2 * heads,)),
                dma((2,)),
                dma,
                dma((3,)),
                dma((heads, 3)),
                dma((3,)),
                dma,
                dma,
                dma,
                pltpu.SemaphoreType.REGULAR((nz // 2,)),
            ],
            compiler_params=pltpu.CompilerParams(
                collective_id=0, has_side_effects=True, vmem_limit_bytes=41943040
            ),
            name="fused",
        )(*[pltpu.with_memory_space_constraint(a, pltpu.HBM) for a in (span_ids, queries[0], keys[0], values[0], cotangent[0])])
        return attention[None], grad[None]

    return jax.shard_map(
        local,
        mesh=mesh,
        in_specs=(
            P("pipe", "ctx", "tp"),
            P("pipe", "ctx", "tp"),
            P("pipe", "ctx", "tp"),
            P("pipe", "ctx"),
            P("pipe", "ctx", None),
        ),
        out_specs=(P("pipe", "ctx", "tp"), P("pipe", "ctx", "tp")),
        check_vma=False,
    )
```
